256 devices in a mesh: dp: 16 (over y_lo, x, core), chan: 16 (over y_hi, z).
Axes of the slice: x: 4, y: 4 (y_hi: 2, y_lo: 2; y = y_hi * 2 + y_lo), z: 8, core: 2. Of those that a mesh axis runs over, the one named last changes fastest.
Arguments:
- anchors: bfloat16 [256, 128, 4096], P('dp', 'chan'), may hold values from -15 to 15
- views: bfloat16 [256, 128, 4096], P('dp', 'chan'), may hold values from -15 to 15
- dw_weight: float32 [128, 4], replicated, may hold values from -3 to 3
- pw_weight: bfloat16 [256, 128], replicated, may hold values from -0.5 to 0.5
- proj_weight: bfloat16 [256, 1024], replicated, may hold values from -0.375 to 0.375
- partner: int32 [256], P('dp'), may hold values from 0 to 255, each once
Outputs:
- loss: float32 [256], P('dp')
- grad_dw: float32 [128, 4], P('chan')
- grad_pw: float32 [256, 128], replicated
- grad_proj: float32 [256, 1024], P('chan', 'dp')
The draws below stay inside these ranges and needn't reach their ends.
Inputs may be any that keep to these rules, and one draw needn't show every extreme that they name: `partner`: each view index appears exactly once.
All inputs are finite; a program needn't handle non-finite values.
Results may differ from the reference program's by a relative error of at most 0.0044.
Values may be sent and summed in bfloat16 or wider, within the bound.
No kernel may reach another device: no remote copies, remote signals or barrier semaphores. Data moves between devices by JAX's collectives and lax.ppermute only.
A program may use at most 192 MiB of HBM per device.

```python
import math
import jax
import jax.numpy as jnp
from jax import lax

METRICS = 128
FILTERS = 256
EMBED = 1024
TRACE_STEPS = 4096
TAPS = 4
TAP_SPACING = 16
ANCHOR_COUNT = 256


def trace_values(key, marker):
    root_key = jax.random.fold_in(key, marker)
    displacement_key, dispersion_key, jitter_key, switch_key, level_jump_key, cycle_length_key, angle_key, sinusoid_key, spike_key = jax.random.split(root_key, 9)
    step_index = jnp.arange(TRACE_STEPS, dtype=jnp.int32)[None, None, :]
    step_positions = step_index.astype(jnp.float32)
    behaviour_mode = jnp.zeros((ANCHOR_COUNT, METRICS, TRACE_STEPS), jnp.float32)
    for shift_index in range(4):
        moment = jax.random.randint(jax.random.fold_in(switch_key, shift_index), (ANCHOR_COUNT, 1, 1), 0, TRACE_STEPS)
        jump = jax.random.uniform(jax.random.fold_in(level_jump_key, shift_index), (ANCHOR_COUNT, METRICS, 1), jnp.float32, -0.75, 0.75)
        behaviour_mode = behaviour_mode + jnp.where(step_index >= moment, jump, 0.0)
    period = TAP_SPACING * jnp.exp(jax.random.uniform(cycle_length_key, (ANCHOR_COUNT, METRICS, 1), jnp.float32, 0.0, jnp.log(32.0)))
    phase = jax.random.uniform(angle_key, (ANCHOR_COUNT, METRICS, 1), jnp.float32, -math.pi, math.pi)
    spike_middle = jax.random.randint(spike_key, (ANCHOR_COUNT, 1, 1), 0, TRACE_STEPS).astype(jnp.float32)
    spike_width = 4.0 * TAP_SPACING
    distance_from_middle = (step_positions - spike_middle) / spike_width
    spike_height = 1.0 + jnp.exp(-distance_from_middle * distance_from_middle)
    level_shift = jnp.clip(jax.random.normal(displacement_key, (ANCHOR_COUNT, METRICS, 1), jnp.float32), -3.0, 3.0)
    dispersion = jnp.exp(jax.random.uniform(dispersion_key, (ANCHOR_COUNT, METRICS, 1), jnp.float32, jnp.log(0.3), jnp.log(3.0)))
    jitter_component = jnp.clip(jax.random.normal(jitter_key, (ANCHOR_COUNT, METRICS, TRACE_STEPS), jnp.float32), -4.0, 4.0)
    wave_size = jax.random.uniform(sinusoid_key, (ANCHOR_COUNT, METRICS, 1), jnp.float32, 0.3, 1.2)
    sinusoid = wave_size * jnp.sin(2.0 * math.pi * step_positions / period + phase)
    signal_samples = level_shift + behaviour_mode + dispersion * (spike_height * jitter_component + sinusoid)
    return jnp.clip(signal_samples, -15.0, 15.0).astype(jnp.bfloat16)


def draw_anchors(key, part):
    return trace_values(key, 11)


def draw_views(key, part):
    return trace_values(key, 23)


def scatter_about(key, shape, width, bound, held_as=jnp.bfloat16):
    array = width * jax.random.normal(key, shape, jnp.float32)
    return jnp.clip(array, min=-bound, max=bound).astype(held_as)


def setup_inputs(seed: int = 0) -> dict:
    streams_of = jax.random.split(jax.random.key(seed), 7)
    return {
        "anchors": draw_anchors(jax.random.fold_in(streams_of[6], 71), 0),
        "views": draw_views(jax.random.fold_in(streams_of[6], 71), 0),
        "dw_weight": scatter_about(streams_of[2], (METRICS, TAPS), TAPS ** -0.5, 3.0, jnp.float32),
        "pw_weight": scatter_about(streams_of[3], (FILTERS, METRICS), METRICS ** -0.5, 0.5),
        "proj_weight": scatter_about(streams_of[4], (FILTERS, EMBED), FILTERS ** -0.5, 0.375),
        "partner": jax.random.permutation(streams_of[5], ANCHOR_COUNT).astype(jnp.int32),
    }


logit_scale = 16.0

def depthwise(trace_block, dw_weight):
    widened = trace_block.astype(jnp.float32)
    length = trace_block.shape[2]
    running = jnp.zeros(widened.shape, jnp.float32)
    for tap_index in range(TAPS):
        offset_steps = tap_index * TAP_SPACING
        shifted = jnp.pad(widened[:, :, :length - offset_steps], ((0, 0), (0, 0), (offset_steps, 0)))
        running = running + dw_weight[None, :, tap_index, None] * shifted
    return running.astype(jnp.bfloat16)

def mixing(conv, pw_weight):
    return jnp.einsum('fc,nct->nft', pw_weight.astype(jnp.float32), conv.astype(jnp.float32))

def silu_slope(mixed):
    sigma = jax.nn.sigmoid(mixed)
    return sigma * (1.0 + mixed * (1.0 - sigma))

def kernel_terms(grad_conv, extended):
    rim_width = (TAPS - 1) * TAP_SPACING
    span_width = grad_conv.shape[2]
    columns = []
    for tap_index in range(TAPS):
        begin = rim_width - tap_index * TAP_SPACING
        window = extended[:, :, begin:begin + span_width]
        columns.append(jnp.einsum('nct,nct->c', grad_conv.astype(jnp.float32), window.astype(jnp.float32)))
    return jnp.stack(columns, 1)

def reference(anchors, views, dw_weight, pw_weight, proj_weight, partner):
    traces = jnp.concatenate([anchors, views], 0)
    total_traces = traces.shape[0]
    block_size = 16
    blocks = traces.reshape(total_traces // block_size, block_size, METRICS, TRACE_STEPS)

    def forward_block(trace_block):
        mixed = mixing(depthwise(trace_block, dw_weight), pw_weight)
        return lax.optimization_barrier(jnp.sum(jax.nn.silu(mixed), 2)) / TRACE_STEPS
    pooled = lax.map(forward_block, blocks).reshape(total_traces, FILTERS)
    pooled_bf = pooled.astype(jnp.bfloat16)
    embedding = jnp.dot(pooled_bf, proj_weight, preferred_element_type=jnp.float32)
    inverse = lax.rsqrt(lax.optimization_barrier(jnp.mean(embedding * embedding, 1, keepdims=True)) + 1e-06)
    unit_rows = embedding * inverse
    unit_bf = unit_rows.astype(jnp.bfloat16)
    queries = unit_bf[:ANCHOR_COUNT]
    key_rows = unit_bf[ANCHOR_COUNT:]
    factor = logit_scale / EMBED
    logits = factor * jnp.dot(queries, key_rows.T, preferred_element_type=jnp.float32)
    weights = jnp.exp(logits - logit_scale)
    totals = lax.optimization_barrier(jnp.sum(weights, 1))
    matches = jnp.arange(ANCHOR_COUNT, dtype=jnp.int32)[None, :] == partner[:, None]
    positive = lax.optimization_barrier(jnp.sum(jnp.where(matches, logits, 0.0), 1))
    losses = logit_scale + jnp.log(totals) - positive
    coeffs = (weights / totals[:, None] - matches.astype(jnp.float32)).astype(jnp.bfloat16)
    grad_query = factor * jnp.dot(coeffs, key_rows, preferred_element_type=jnp.float32)
    grad_key = factor * jnp.dot(coeffs.T, queries, preferred_element_type=jnp.float32)
    grad_unit = jnp.concatenate([grad_query, grad_key], 0)
    grad_embed = inverse * (grad_unit - unit_rows * lax.optimization_barrier(jnp.mean(unit_rows * grad_unit, 1, keepdims=True)))
    grad_embed_bf = grad_embed.astype(jnp.bfloat16)
    grad_proj = jnp.dot(pooled_bf.T, grad_embed_bf, preferred_element_type=jnp.float32)
    grad_pool = jnp.dot(grad_embed_bf, proj_weight.T, preferred_element_type=jnp.float32)
    pool_blocks = grad_pool.reshape(total_traces // block_size, block_size, FILTERS)
    rim_width = (TAPS - 1) * TAP_SPACING

    def backward_block(sums, inputs):
        trace_block, pool_block = inputs
        conv = depthwise(trace_block, dw_weight)
        mixed = mixing(conv, pw_weight)
        grad_mixed = (pool_block[:, :, None] / TRACE_STEPS * silu_slope(mixed)).astype(jnp.bfloat16)
        mix_terms = jnp.einsum('nft,nct->fc', grad_mixed.astype(jnp.float32), conv.astype(jnp.float32))
        grad_conv = jnp.einsum('fc,nft->nct', pw_weight.astype(jnp.float32), grad_mixed.astype(jnp.float32)).astype(jnp.bfloat16)
        extended = jnp.pad(trace_block, ((0, 0), (0, 0), (rim_width, 0)))
        return ((sums[0] + mix_terms, sums[1] + kernel_terms(grad_conv, extended)), None)
    start_sums = (jnp.zeros((FILTERS, METRICS), jnp.float32), jnp.zeros((METRICS, TAPS), jnp.float32))
    sums, unused = lax.scan(backward_block, start_sums, (blocks, pool_blocks))
    return (losses, sums[1], sums[0], grad_proj)
```

```python
import functools

import jax
import jax.numpy as jnp
from jax import lax
from jax.experimental import pallas as pl
from jax.experimental.pallas import tpu as pltpu
from jax.sharding import PartitionSpec as P

TAPS = 4
TAP_SPACING = 16
LANES = 128
LOGIT_SCALE = 16.0
CHUNK = 1024
ROWS = 32
F32 = jnp.float32
BF16 = jnp.bfloat16


def trace_kernel(length, x_ref, halo_ref, dw_ref, pw_ref, pool_ref, terms_ref, mixed, slope, taps, acc):
    step = pl.program_id(0)
    metrics, chunk = x_ref.shape
    filters = pw_ref.shape[0]

    @pl.when(step == 0)
    def _():
        acc[...] = jnp.zeros_like(acc)
        terms_ref[...] = jnp.zeros_like(terms_ref)

    for begin in range(0, metrics, ROWS):
        rows = pl.ds(begin, ROWS)
        block = x_ref[rows, :].astype(F32)
        halo = halo_ref[rows, :].astype(F32)
        halo = jnp.where(step > 0, halo, jnp.zeros_like(halo))
        extended = jnp.concatenate([halo, block], axis=1)
        kernel = dw_ref[rows, :]
        running = kernel[:, 0:1] * block
        taps[pl.ds(metrics + begin, ROWS), :] = x_ref[rows, :]
        for tap in range(1, TAPS):
            shifted = pltpu.roll(extended, tap * TAP_SPACING, 1)[:, LANES:]
            running = running + kernel[:, tap : tap + 1] * shifted
            taps[pl.ds(metrics * (tap + 1) + begin, ROWS), :] = shifted.astype(BF16)
        taps[rows, :] = running.astype(BF16)

    mixed[...] = jnp.dot(pw_ref[...], taps[pl.ds(0, metrics), :], preferred_element_type=F32)

    def activate(index, carry):
        rows = pl.ds(pl.multiple_of(index * ROWS, ROWS), ROWS)
        value = mixed[rows, :]
        sigma = jax.nn.sigmoid(value)
        silu = value * sigma
        slope[rows, :] = (sigma + silu * (1.0 - sigma)).astype(BF16)
        total = silu[:, 0:LANES]
        for lane in range(LANES, chunk, LANES):
            total = total + silu[:, lane : lane + LANES]
        acc[rows, :] = acc[rows, :] + total
        return carry

    lax.fori_loop(0, filters // ROWS, activate, 0)
    terms_ref[...] += lax.dot_general(
        taps[...], slope[...], (((1,), (1,)), ((), ())), preferred_element_type=F32
    )

    @pl.when(step == pl.num_programs(0) - 1)
    def _():
        turned = acc[...].T
        pool_ref[...] = jnp.sum(turned, 0, keepdims=True) / length


def trace_pass(trace, dw_weight, pw_weight):
    metrics, length = trace.shape
    filters = pw_weight.shape[0]
    chunk = CHUNK
    per_halo = chunk // LANES
    return pl.pallas_call(
        functools.partial(trace_kernel, length),
        grid=(length // chunk,),
        in_specs=[
            pl.BlockSpec((metrics, chunk), lambda i: (0, i)),
            pl.BlockSpec((metrics, LANES), lambda i: (0, jnp.maximum(i * per_halo - 1, 0))),
            pl.BlockSpec((metrics, TAPS), lambda i: (0, 0)),
            pl.BlockSpec((filters, metrics), lambda i: (0, 0)),
        ],
        out_specs=[
            pl.BlockSpec((1, filters), lambda i: (0, 0)),
            pl.BlockSpec((metrics * (TAPS + 1), filters), lambda i: (0, 0)),
        ],
        out_shape=[
            jax.ShapeDtypeStruct((1, filters), F32),
            jax.ShapeDtypeStruct((metrics * (TAPS + 1), filters), F32),
        ],
        scratch_shapes=[
            pltpu.VMEM((filters, chunk), F32),
            pltpu.VMEM((filters, chunk), BF16),
            pltpu.VMEM((metrics * (TAPS + 1), chunk), BF16),
            pltpu.VMEM((filters, LANES), F32),
        ],
        compiler_params=pltpu.CompilerParams(
            dimension_semantics=("arbitrary",), vmem_limit_bytes=40 << 20
        ),
    )(trace, trace, dw_weight, pw_weight)


def middle_kernel(
    length, own_ref, pooled_ref, proj_ref, pw_turned_ref, terms_a_ref, terms_v_ref,
    loss_ref, grad_a_ref, grad_v_ref, sums_ref, held_a, held_v,
):
    filters, width = proj_ref.shape
    count = pooled_ref.shape[0]
    metrics = pw_turned_ref.shape[0]
    factor = LOGIT_SCALE / width
    proj = proj_ref[...]

    def normed(pooled):
        embedding = jnp.dot(pooled, proj, preferred_element_type=F32)
        inverse = lax.rsqrt(jnp.mean(embedding * embedding, 1, keepdims=True) + 1e-06)
        return embedding * inverse, inverse

    unit_a, inverse_a = normed(pooled_ref[:, 0:filters])
    unit_v, inverse_v = normed(pooled_ref[:, filters : 2 * filters])
    queries = unit_a.astype(BF16)
    keys = unit_v.astype(BF16)
    logits = factor * lax.dot_general(
        queries, keys, (((1,), (1,)), ((), ())), preferred_element_type=F32
    )
    partner = pooled_ref[:, 2 * filters : 2 * filters + 1].astype(F32).astype(jnp.int32)
    columns = lax.broadcasted_iota(jnp.int32, (count, count), 1)
    matches = columns == partner
    weights = jnp.exp(logits - LOGIT_SCALE)
    totals = jnp.sum(weights, 1, keepdims=True)
    positive = jnp.sum(jnp.where(matches, logits, 0.0), 1, keepdims=True)
    loss_ref[...] = LOGIT_SCALE + jnp.log(totals) - positive
    coeffs = (weights / totals - jnp.where(matches, 1.0, 0.0)).astype(BF16)
    unit_grad_a = factor * jnp.dot(coeffs, keys, preferred_element_type=F32)
    unit_grad_v = factor * lax.dot_general(
        coeffs, queries, (((0,), (0,)), ((), ())), preferred_element_type=F32
    )

    def embed_grad(unit, inverse, unit_grad):
        return inverse * (unit_grad - unit * jnp.mean(unit * unit_grad, 1, keepdims=True))

    own = own_ref[0]

    def pool_grad(unit, inverse, unit_grad, out_ref, held):
        grad = embed_grad(unit, inverse, unit_grad).astype(BF16)
        out_ref[...] = grad
        held[...] = grad.astype(F32)
        row = jnp.broadcast_to(held[pl.ds(own, 1), :], (16, width)).astype(BF16)
        pool = lax.dot_general(row, proj, (((1,), (1,)), ((), ())), preferred_element_type=F32)
        return pool[0:1, :] / length

    pool_a = pool_grad(unit_a, inverse_a, unit_grad_a, grad_a_ref, held_a)
    pool_v = pool_grad(unit_v, inverse_v, unit_grad_v, grad_v_ref, held_v)

    def weighted(index):
        rows = pl.ds(index * metrics, metrics)
        return terms_a_ref[rows, :] * pool_a + terms_v_ref[rows, :] * pool_v

    mixing = weighted(0).T
    pw_turned = pw_turned_ref[...].astype(F32)
    lanes = lax.broadcasted_iota(jnp.int32, (metrics, LANES), 1)
    kernel = jnp.zeros((metrics, LANES), F32)
    for tap in range(TAPS):
        column = jnp.sum(pw_turned * weighted(tap + 1), 1, keepdims=True)
        kernel = kernel + jnp.where(lanes == tap, column, 0.0)
    parts = sums_ref.shape[0]
    mix_rows, tap_rows = filters // parts, metrics // parts
    for part in range(parts):
        sums_ref[part, 0:mix_rows, :] = mixing[part * mix_rows : (part + 1) * mix_rows, :]
        sums_ref[part, mix_rows : mix_rows + tap_rows, :] = kernel[
            part * tap_rows : (part + 1) * tap_rows, :
        ]


def middle(own, pooled, proj_weight, pw_turned, terms_a, terms_v, parts, length):
    filters, width = proj_weight.shape
    metrics = pw_turned.shape[0]
    count = pooled.shape[0]
    whole = pl.BlockSpec(memory_space=pltpu.VMEM)
    rows = filters // parts + metrics // parts
    return pl.pallas_call(
        functools.partial(middle_kernel, length),
        in_specs=[pl.BlockSpec(memory_space=pltpu.SMEM)] + [whole] * 5,
        out_specs=[whole] * 4,
        out_shape=[
            jax.ShapeDtypeStruct((count, 1), F32),
            jax.ShapeDtypeStruct((count, width), BF16),
            jax.ShapeDtypeStruct((count, width), BF16),
            jax.ShapeDtypeStruct((parts, rows, metrics), F32),
        ],
        scratch_shapes=[pltpu.VMEM((count, width), F32), pltpu.VMEM((count, width), F32)],
        compiler_params=pltpu.CompilerParams(vmem_limit_bytes=48 << 20),
    )(own, pooled, proj_weight, pw_turned, terms_a, terms_v)


def swap(value, axis):
    return lax.all_to_all(value, axis, 0, 0, tiled=True)


def spread(value, axis):
    count = lax.axis_size(axis)
    return swap(jnp.broadcast_to(value[None], (count,) + value.shape), axis)


def body(anchors, views, dw_weight, pw_weight, proj_weight, partner):
    chan_index = lax.axis_index("chan")
    dp_index = lax.axis_index("dp")
    chan_count = lax.axis_size("chan")
    dp_count = lax.axis_size("dp")
    pairs, local_metrics, length = anchors.shape
    filters, metrics = pw_weight.shape
    width = proj_weight.shape[1]

    trace_a = swap(anchors, "chan").reshape(metrics, length)
    trace_v = swap(views, "chan").reshape(metrics, length)
    pool_a, terms_a = trace_pass(trace_a, dw_weight, pw_weight)
    pool_v, terms_v = trace_pass(trace_v, dw_weight, pw_weight)
    own_partner = lax.dynamic_slice_in_dim(partner, chan_index, 1, 0).astype(BF16)
    message = jnp.concatenate(
        [pool_a.astype(BF16), pool_v.astype(BF16), jnp.broadcast_to(own_partner[None], (1, LANES))], 1
    )
    pooled = spread(message, ("dp", "chan")).reshape(dp_count * chan_count, message.shape[1])

    own = (dp_index * chan_count + chan_index).astype(jnp.int32).reshape(1)
    losses, grad_a, grad_v, sums = middle(
        own, pooled, proj_weight, pw_weight.T, terms_a, terms_v, chan_count, length
    )

    summed = jnp.sum(swap(sums, "chan"), 0)
    summed = jnp.sum(spread(summed, "dp"), 0)
    mix_rows = filters // chan_count
    grad_dw = summed[mix_rows:, :TAPS]
    grad_pw = spread(summed[:mix_rows], "chan").reshape(filters, metrics)

    cols = width // dp_count
    rows = filters // chan_count

    def proj_part(offset, grad):
        features = lax.dynamic_slice_in_dim(pooled, offset + chan_index * rows, rows, 1)
        part = lax.dynamic_slice_in_dim(grad, dp_index * cols, cols, 1)
        return lax.dot_general(
            features, part, (((0,), (0,)), ((), ())), preferred_element_type=F32
        )

    grad_proj = proj_part(0, grad_a) + proj_part(filters, grad_v)
    loss = lax.dynamic_slice_in_dim(losses, dp_index * pairs, pairs, 0).reshape(pairs)
    return (loss, grad_dw, grad_pw, grad_proj)


def solution(mesh):
    placed = (P("dp", "chan", None), P("dp", "chan", None), P(), P(), P(), P("dp"))
    return jax.shard_map(
        body,
        mesh=mesh,
        in_specs=placed,
        out_specs=(P("dp"), P("chan", None), P(), P("chan", "dp")),
        check_vma=False,
    )
```

```python
import functools

import jax
import jax.numpy as jnp
from jax import lax
from jax.experimental import pallas as pl
from jax.experimental.pallas import tpu as pltpu
from jax.sharding import PartitionSpec as P

TAPS = 4
TAP_SPACING = 16
LANES = 128
LOGIT_SCALE = 16.0
POOL_CHUNK = 1024
TERM_CHUNK = 1024
ROWS = 32
F32 = jnp.float32
BF16 = jnp.bfloat16


def convolved(x_ref, halo_ref, dw_ref, begin, step, keep=None):
    sources = ROWS // x_ref.shape[2]
    first = begin // x_ref.shape[2]
    block = x_ref[first : first + sources, 0].astype(F32).reshape(ROWS, x_ref.shape[3])
    halo = halo_ref[first : first + sources, 0].astype(F32).reshape(ROWS, LANES)
    halo = jnp.where(step > 0, halo, jnp.zeros_like(halo))
    extended = jnp.concatenate([halo, block], axis=1)
    kernel = dw_ref[begin : begin + ROWS, :]
    running = kernel[:, 0:1] * block
    if keep is not None:
        keep(0, block)
    for tap in range(1, TAPS):
        shifted = pltpu.roll(extended, tap * TAP_SPACING, 1)[:, LANES:]
        running = running + kernel[:, tap : tap + 1] * shifted
        if keep is not None:
            keep(tap, shifted)
    return running.astype(BF16)


def pool_kernel(length, own_ref, x_ref, halo_ref, dw_ref, pw_ref, message_ref, conv, half, acc, rows_held):
    trace, step = pl.program_id(0), pl.program_id(1)
    metrics = dw_ref.shape[0]
    filters, chunk = half.shape

    @pl.when(step == 0)
    def _():
        acc[...] = jnp.zeros_like(acc)

    for begin in range(0, metrics, ROWS):
        conv[pl.ds(begin, ROWS), :] = convolved(x_ref, halo_ref, dw_ref, begin, step)
    half[...] = jnp.dot(pw_ref[...] * 0.5, conv[...], preferred_element_type=F32)

    def activate(index, carry):
        rows = pl.ds(pl.multiple_of(index * ROWS, ROWS), ROWS)
        value = half[rows, :]
        silu = value + value * jnp.tanh(value)
        total = silu[:, 0:LANES]
        for lane in range(LANES, chunk, LANES):
            total = total + silu[:, lane : lane + LANES]
        acc[rows, :] = acc[rows, :] + total
        return carry

    lax.fori_loop(0, filters // ROWS, activate, 0)

    @pl.when(step == pl.num_programs(1) - 1)
    def _():
        pooled = jnp.sum(acc[...].T, 0, keepdims=True) / length
        rows_held[pl.ds(trace, 1), :] = pooled

    @pl.when((step == pl.num_programs(1) - 1) & (trace == pl.num_programs(0) - 1))
    def _():
        mark = jnp.full((2, LANES), own_ref[1], jnp.int32).astype(F32)
        row = jnp.concatenate([rows_held[0:2, :], mark], 1).astype(BF16)
        message_ref[...] = jnp.broadcast_to(row[None], message_ref.shape)


def terms_kernel(x_ref, halo_ref, dw_ref, pw_ref, proj_ref, terms_ref, proj_out_ref, half, slope, taps):
    trace, step = pl.program_id(0), pl.program_id(1)
    metrics = dw_ref.shape[0]
    filters, chunk = half.shape

    @pl.when(step == 0)
    def _():
        terms_ref[...] = jnp.zeros_like(terms_ref)

    @pl.when((step == 0) & (trace == 0))
    def _():
        proj_out_ref[...] = proj_ref[...]

    for begin in range(0, metrics, ROWS):

        def keep(tap, shifted):
            taps[pl.ds(metrics * (tap + 1) + begin, ROWS), :] = shifted.astype(BF16)

        taps[pl.ds(begin, ROWS), :] = convolved(x_ref, halo_ref, dw_ref, begin, step, keep)
    half[...] = jnp.dot(pw_ref[...] * 0.5, taps[0:metrics, :], preferred_element_type=F32)

    def activate(index, carry):
        rows = pl.ds(pl.multiple_of(index * ROWS, ROWS), ROWS)
        value = half[rows, :]
        turn = jnp.tanh(value)
        slope[rows, :] = ((1.0 + turn) * (1.0 + value * (1.0 - turn))).astype(BF16)
        return carry

    lax.fori_loop(0, filters // ROWS, activate, 0)
    terms_ref[0] += lax.dot_general(
        taps[...], slope[...], (((1,), (1,)), ((), ())), preferred_element_type=F32
    )


def trace_specs(traces, filters, chunk):
    sources, pair, local, length = traces.shape
    per_halo = chunk // LANES
    return [
        pl.BlockSpec((sources, 1, local, chunk), lambda n, i: (0, n, 0, i)),
        pl.BlockSpec(
            (sources, 1, local, LANES), lambda n, i: (0, n, 0, jnp.maximum(i * per_halo - 1, 0))
        ),
        pl.BlockSpec((sources * local, TAPS), lambda n, i: (0, 0)),
        pl.BlockSpec((filters, sources * local), lambda n, i: (0, 0)),
    ]


def pool_pass(own, traces, dw_weight, pw_weight, devices):
    sources, pair, local, length = traces.shape
    filters, metrics = pw_weight.shape
    chunk = POOL_CHUNK
    width = filters + LANES
    return pl.pallas_call(
        functools.partial(pool_kernel, length),
        grid=(pair, length // chunk),
        in_specs=[pl.BlockSpec(memory_space=pltpu.SMEM)] + trace_specs(traces, filters, chunk),
        out_specs=pl.BlockSpec((devices, pair, width), lambda n, i: (0, 0, 0)),
        out_shape=jax.ShapeDtypeStruct((devices, pair, width), BF16),
        scratch_shapes=[
            pltpu.VMEM((metrics, chunk), BF16),
            pltpu.VMEM((filters, chunk), F32),
            pltpu.VMEM((filters, LANES), F32),
            pltpu.VMEM((8, filters), F32),
        ],
        compiler_params=pltpu.CompilerParams(
            dimension_semantics=("arbitrary", "arbitrary"), vmem_limit_bytes=32 << 20
        ),
    )(own, traces, traces, dw_weight, pw_weight)


def terms_pass(traces, dw_weight, pw_weight, proj_weight):
    sources, pair, local, length = traces.shape
    filters, metrics = pw_weight.shape
    chunk = TERM_CHUNK
    deep = metrics * (TAPS + 1)
    return pl.pallas_call(
        terms_kernel,
        grid=(pair, length // chunk),
        in_specs=trace_specs(traces, filters, chunk)
        + [pl.BlockSpec(proj_weight.shape, lambda n, i: (0, 0))],
        out_specs=[
            pl.BlockSpec((1, deep, filters), lambda n, i: (n, 0, 0)),
            pl.BlockSpec(proj_weight.shape, lambda n, i: (0, 0)),
        ],
        out_shape=[
            jax.ShapeDtypeStruct((pair, deep, filters), F32),
            jax.ShapeDtypeStruct(proj_weight.shape, proj_weight.dtype),
        ],
        scratch_shapes=[
            pltpu.VMEM((filters, chunk), F32),
            pltpu.VMEM((filters, chunk), BF16),
            pltpu.VMEM((deep, chunk), BF16),
        ],
        compiler_params=pltpu.CompilerParams(
            dimension_semantics=("arbitrary", "arbitrary"), vmem_limit_bytes=32 << 20
        ),
    )(traces, traces, dw_weight, pw_weight, proj_weight)


def middle_kernel(
    length, own_ref, pooled_ref, proj_ref, pw_turned_ref, terms_ref,
    loss_ref, grad_a_ref, grad_v_ref, sums_ref, held_a, held_v,
):
    filters, width = proj_ref.shape
    count = pooled_ref.shape[0]
    metrics = pw_turned_ref.shape[0]
    factor = LOGIT_SCALE / width
    proj = proj_ref[...]

    def normed(pooled):
        embedding = jnp.dot(pooled, proj, preferred_element_type=F32)
        inverse = lax.rsqrt(jnp.mean(embedding * embedding, 1, keepdims=True) + 1e-06)
        return embedding * inverse, inverse

    unit_a, inverse_a = normed(pooled_ref[:, 0:filters])
    unit_v, inverse_v = normed(pooled_ref[:, filters + LANES : 2 * filters + LANES])
    queries = unit_a.astype(BF16)
    keys = unit_v.astype(BF16)
    logits = factor * lax.dot_general(
        queries, keys, (((1,), (1,)), ((), ())), preferred_element_type=F32
    )
    partner = pooled_ref[:, filters : filters + 1].astype(F32).astype(jnp.int32)
    columns = lax.broadcasted_iota(jnp.int32, (count, count), 1)
    matches = columns == partner
    weights = jnp.exp(logits - LOGIT_SCALE)
    totals = jnp.sum(weights, 1, keepdims=True)
    positive = jnp.sum(jnp.where(matches, logits, 0.0), 1, keepdims=True)
    loss_ref[...] = LOGIT_SCALE + jnp.log(totals) - positive
    coeffs = (weights / totals - jnp.where(matches, 1.0, 0.0)).astype(BF16)
    unit_grad_a = factor * jnp.dot(coeffs, keys, preferred_element_type=F32)
    unit_grad_v = factor * lax.dot_general(
        coeffs, queries, (((0,), (0,)), ((), ())), preferred_element_type=F32
    )

    def embed_grad(unit, inverse, unit_grad):
        return inverse * (unit_grad - unit * jnp.mean(unit * unit_grad, 1, keepdims=True))

    own = own_ref[0]

    def pool_grad(unit, inverse, unit_grad, out_ref, held):
        grad = embed_grad(unit, inverse, unit_grad).astype(BF16)
        out_ref[...] = grad
        held[...] = grad.astype(F32)
        row = jnp.broadcast_to(held[pl.ds(own, 1), :], (16, width)).astype(BF16)
        pool = lax.dot_general(row, proj, (((1,), (1,)), ((), ())), preferred_element_type=F32)
        return pool[0:1, :] * (0.5 / length)

    pool_a = pool_grad(unit_a, inverse_a, unit_grad_a, grad_a_ref, held_a)
    pool_v = pool_grad(unit_v, inverse_v, unit_grad_v, grad_v_ref, held_v)

    def weighted(index):
        rows = pl.ds(index * metrics, metrics)
        return terms_ref[0, rows, :] * pool_a + terms_ref[1, rows, :] * pool_v

    mixing = weighted(0).T
    pw_turned = pw_turned_ref[...].astype(F32)
    lanes = lax.broadcasted_iota(jnp.int32, (metrics, LANES), 1)
    kernel = jnp.zeros((metrics, LANES), F32)
    for tap in range(TAPS):
        column = jnp.sum(pw_turned * weighted(tap + 1), 1, keepdims=True)
        kernel = kernel + jnp.where(lanes == tap, column, 0.0)
    parts = sums_ref.shape[0]
    mix_rows, tap_rows = filters // parts, metrics // parts
    for part in range(parts):
        sums_ref[part, 0:mix_rows, :] = mixing[part * mix_rows : (part + 1) * mix_rows, :]
        sums_ref[part, mix_rows : mix_rows + tap_rows, :] = kernel[
            part * tap_rows : (part + 1) * tap_rows, :
        ]


def middle(own, pooled, proj_weight, pw_turned, terms, parts, length):
    filters, width = proj_weight.shape
    metrics = pw_turned.shape[0]
    count = pooled.shape[0]
    whole = pl.BlockSpec(memory_space=pltpu.VMEM)
    rows = filters // parts + metrics // parts
    return pl.pallas_call(
        functools.partial(middle_kernel, length),
        in_specs=[pl.BlockSpec(memory_space=pltpu.SMEM)] + [whole] * 4,
        out_specs=[whole] * 4,
        out_shape=[
            jax.ShapeDtypeStruct((count, 1), F32),
            jax.ShapeDtypeStruct((count, width), BF16),
            jax.ShapeDtypeStruct((count, width), BF16),
            jax.ShapeDtypeStruct((parts, rows, metrics), F32),
        ],
        scratch_shapes=[pltpu.VMEM((count, width), F32), pltpu.VMEM((count, width), F32)],
        compiler_params=pltpu.CompilerParams(vmem_limit_bytes=48 << 20),
    )(own, pooled, proj_weight, pw_turned, terms)


def swap(value, axis):
    return lax.all_to_all(value, axis, 0, 0, tiled=True)


def fold_kernel(mix_rows, parts_ref, out_ref, tap_ref=None):
    total = jnp.sum(parts_ref[...], 0)
    if tap_ref is not None:
        tap_ref[...] = total[mix_rows:, 0:TAPS]
        total = total[0:mix_rows, :]
    out_ref[...] = jnp.broadcast_to(total[None], out_ref.shape)


def fold(parts, mix_rows, last):
    count, rows, width = parts.shape
    whole = pl.BlockSpec(memory_space=pltpu.VMEM)
    out = jax.ShapeDtypeStruct((count, mix_rows if last else rows, width), F32)
    if last:
        out = [out, jax.ShapeDtypeStruct((rows - mix_rows, TAPS), F32)]
    return pl.pallas_call(
        functools.partial(fold_kernel, mix_rows),
        in_specs=[whole],
        out_specs=[whole] * 2 if last else whole,
        out_shape=out,
    )(parts)


def body(anchors, views, dw_weight, pw_weight, proj_weight, partner):
    chan_index = lax.axis_index("chan")
    dp_index = lax.axis_index("dp")
    chan_count = lax.axis_size("chan")
    dp_count = lax.axis_size("dp")
    pairs, local_metrics, length = anchors.shape
    filters, metrics = pw_weight.shape
    width = proj_weight.shape[1]

    position = (dp_index * chan_count + chan_index).astype(jnp.int32)
    own = jnp.stack([position, lax.dynamic_slice_in_dim(partner, chan_index, 1, 0)[0]])
    traces = swap(jnp.stack([anchors, views], 1), "chan")
    message = pool_pass(own, traces, dw_weight, pw_weight, dp_count * chan_count)
    pooled = swap(message, ("dp", "chan")).reshape(message.shape[0], -1)
    terms, proj_held = terms_pass(traces, dw_weight, pw_weight, proj_weight)
    losses, grad_a, grad_v, sums = middle(
        own, pooled, proj_held, pw_weight.T, terms, chan_count, length
    )

    folded = fold(swap(sums, "chan"), filters // chan_count, False)
    shares, grad_dw = fold(swap(folded, "dp"), filters // chan_count, True)
    grad_pw = swap(shares, "chan").reshape(filters, metrics)

    cols = width // dp_count
    rows = filters // chan_count

    def proj_part(offset, grad):
        features = lax.dynamic_slice_in_dim(pooled, offset + chan_index * rows, rows, 1)
        part = lax.dynamic_slice_in_dim(grad, dp_index * cols, cols, 1)
        return lax.dot_general(
            features, part, (((0,), (0,)), ((), ())), preferred_element_type=F32
        )

    grad_proj = proj_part(0, grad_a) + proj_part(filters + LANES, grad_v)
    loss = lax.dynamic_slice_in_dim(losses, dp_index * pairs, pairs, 0).reshape(pairs)
    return (loss, grad_dw, grad_pw, grad_proj)


def solution(mesh):
    placed = (P("dp", "chan", None), P("dp", "chan", None), P(), P(), P(), P("dp"))
    return jax.shard_map(
        body,
        mesh=mesh,
        in_specs=placed,
        out_specs=(P("dp"), P("chan", None), P(), P("chan", "dp")),
        check_vma=False,
    )
```

```python
import functools

import jax
import jax.numpy as jnp
from jax import lax
from jax.experimental import pallas as pl
from jax.experimental.pallas import tpu as pltpu
from jax.sharding import PartitionSpec as P

TAPS = 4
TAP_SPACING = 16
RIM = (TAPS - 1) * TAP_SPACING
LOGIT_SCALE = 16.0
LANES = 128
SUBLANES = 8
POOL_CHUNK = 2048
BLOCK = 128
F32 = jnp.float32
BF16 = jnp.bfloat16


def mixed_half(block, begin, dw_turned_ref, half_turned, turned):
    steps = block.shape[1]
    flipped = block.T
    turned[RIM + begin : RIM + begin + steps, :] = flipped
    running = dw_turned_ref[0:1, :] * flipped
    for tap in range(1, TAPS):
        first = RIM + begin - tap * TAP_SPACING
        running = running + dw_turned_ref[tap : tap + 1, :] * turned[first : first + steps, :]
    return jnp.dot(running.astype(BF16), half_turned, preferred_element_type=F32)


def pool_kernel(length, x_ref, dw_turned_ref, pw_turned_ref, message_ref, turned, acc, held):
    trace, step = pl.program_id(0), pl.program_id(1)
    sources, _, local, chunk = x_ref.shape
    filters = pw_turned_ref.shape[1]

    @pl.when(step == 0)
    def _():
        acc[...] = jnp.zeros_like(acc)
        turned[0:RIM, :] = jnp.zeros((RIM, sources * local), F32)

    @pl.when(step > 0)
    def _():
        turned[0:RIM, :] = turned[chunk : chunk + RIM, :]

    half_turned = pw_turned_ref[...] * 0.5
    total = acc[...]
    for begin in range(0, chunk, BLOCK):
        block = x_ref[:, 0, :, begin : begin + BLOCK].astype(F32).reshape(sources * local, BLOCK)
        value = mixed_half(block, begin, dw_turned_ref, half_turned, turned)
        silu = value + value * jnp.tanh(value)
        total = total + jnp.sum(silu.reshape(BLOCK // SUBLANES, SUBLANES, filters), 0)
    acc[...] = total

    @pl.when(step == pl.num_programs(1) - 1)
    def _():
        held[pl.ds(trace, 1), :] = jnp.sum(acc[...], 0, keepdims=True) / length

    @pl.when((step == pl.num_programs(1) - 1) & (trace == pl.num_programs(0) - 1))
    def _():
        rows = held[0 : message_ref.shape[1], :].astype(BF16)
        message_ref[...] = jnp.broadcast_to(rows[None], message_ref.shape)


def pool_pass(traces, dw_turned, pw_turned, devices):
    sources, pair, local, length = traces.shape
    metrics, filters = pw_turned.shape
    return pl.pallas_call(
        functools.partial(pool_kernel, length),
        grid=(pair, length // POOL_CHUNK),
        in_specs=[
            pl.BlockSpec((sources, 1, local, POOL_CHUNK), lambda n, i: (0, n, 0, i)),
            pl.BlockSpec(dw_turned.shape, lambda n, i: (0, 0)),
            pl.BlockSpec(pw_turned.shape, lambda n, i: (0, 0)),
        ],
        out_specs=pl.BlockSpec((devices, pair, filters), lambda n, i: (0, 0, 0)),
        out_shape=jax.ShapeDtypeStruct((devices, pair, filters), BF16),
        scratch_shapes=[
            pltpu.VMEM((POOL_CHUNK + RIM, metrics), F32),
            pltpu.VMEM((SUBLANES, filters), F32),
            pltpu.VMEM((SUBLANES, filters), F32),
        ],
        compiler_params=pltpu.CompilerParams(
            dimension_semantics=("arbitrary", "arbitrary"), vmem_limit_bytes=12 << 20
        ),
    )(traces, dw_turned, pw_turned)


def terms_kernel(
    x_ref, dw_turned_ref, pw_turned_ref, terms_ref, turned, slope, plain
):
    sources, _, local, length = x_ref.shape
    metrics = sources * local
    half_turned = pw_turned_ref[...] * 0.5
    turned[0:RIM, :] = jnp.zeros((RIM, metrics), F32)
    slope[length : length + RIM, :] = jnp.zeros((RIM, slope.shape[1]), BF16)
    for begin in range(0, length, BLOCK):
        block = x_ref[:, 0, :, begin : begin + BLOCK].astype(F32).reshape(metrics, BLOCK)
        plain[:, begin : begin + BLOCK] = block.astype(BF16)
        value = mixed_half(block, begin, dw_turned_ref, half_turned, turned)
        bent = jnp.tanh(value)
        slope[begin : begin + BLOCK, :] = (
            (1.0 + bent) * (1.0 + value * (1.0 - bent))
        ).astype(BF16)
    for tap in range(TAPS):
        first = tap * TAP_SPACING
        terms_ref[0, tap * metrics : (tap + 1) * metrics, :] = jnp.dot(
            plain[...], slope[first : first + length, :], preferred_element_type=F32
        )


def terms_pass(traces, dw_turned, pw_turned):
    sources, pair, local, length = traces.shape
    metrics, filters = pw_turned.shape
    return pl.pallas_call(
        terms_kernel,
        grid=(pair,),
        in_specs=[
            pl.BlockSpec((sources, 1, local, length), lambda n: (0, n, 0, 0)),
            pl.BlockSpec(dw_turned.shape, lambda n: (0, 0)),
            pl.BlockSpec(pw_turned.shape, lambda n: (0, 0)),
        ],
        out_specs=pl.BlockSpec((1, metrics * TAPS, filters), lambda n: (n, 0, 0)),
        out_shape=jax.ShapeDtypeStruct((pair, metrics * TAPS, filters), F32),
        scratch_shapes=[
            pltpu.VMEM((length + RIM, metrics), F32),
            pltpu.VMEM((length + RIM, filters), BF16),
            pltpu.VMEM((metrics, length), BF16),
        ],
        compiler_params=pltpu.CompilerParams(
            dimension_semantics=("arbitrary",), vmem_limit_bytes=20 << 20
        ),
    )(traces, dw_turned, pw_turned)


def middle_kernel(
    length, own_ref, pooled_ref, partner_ref, proj_ref, dw_ref, pw_turned_ref, terms_ref,
    loss_ref, grad_a_ref, grad_v_ref, sums_ref, held_a, held_v,
):
    filters, width = proj_ref.shape
    count = pooled_ref.shape[0]
    metrics = pw_turned_ref.shape[0]
    factor = LOGIT_SCALE / width
    proj = proj_ref[...]

    def normed(pooled):
        embedding = jnp.dot(pooled, proj, preferred_element_type=F32)
        inverse = lax.rsqrt(jnp.mean(embedding * embedding, 1, keepdims=True) + 1e-06)
        return embedding * inverse, inverse

    unit_a, inverse_a = normed(pooled_ref[:, 0:filters])
    unit_v, inverse_v = normed(pooled_ref[:, filters : 2 * filters])
    queries = unit_a.astype(BF16)
    keys = unit_v.astype(BF16)
    logits = factor * lax.dot_general(
        queries, keys, (((1,), (1,)), ((), ())), preferred_element_type=F32
    )
    columns = lax.broadcasted_iota(jnp.int32, (count, count), 1)
    matches = columns == partner_ref[...]
    weights = jnp.exp(logits - LOGIT_SCALE)
    totals = jnp.sum(weights, 1, keepdims=True)
    positive = jnp.sum(jnp.where(matches, logits, 0.0), 1, keepdims=True)
    loss_ref[...] = LOGIT_SCALE + jnp.log(totals) - positive
    coeffs = (weights / totals - jnp.where(matches, 1.0, 0.0)).astype(BF16)
    unit_grad_a = factor * jnp.dot(coeffs, keys, preferred_element_type=F32)
    unit_grad_v = factor * lax.dot_general(
        coeffs, queries, (((0,), (0,)), ((), ())), preferred_element_type=F32
    )
    own = own_ref[0]

    def pool_grad(unit, inverse, unit_grad, out_ref, held):
        grad = inverse * (unit_grad - unit * jnp.mean(unit * unit_grad, 1, keepdims=True))
        grad = grad.astype(BF16)
        out_ref[...] = grad
        held[...] = grad.astype(F32)
        row = jnp.broadcast_to(held[pl.ds(own, 1), :], (16, width)).astype(BF16)
        pool = lax.dot_general(row, proj, (((1,), (1,)), ((), ())), preferred_element_type=F32)
        return pool[0:1, :] * (0.5 / length)

    pool_a = pool_grad(unit_a, inverse_a, unit_grad_a, grad_a_ref, held_a)
    pool_v = pool_grad(unit_v, inverse_v, unit_grad_v, grad_v_ref, held_v)

    pw_turned = pw_turned_ref[...].astype(F32)
    lanes = lax.broadcasted_iota(jnp.int32, (metrics, LANES), 1)
    mixing = jnp.zeros((metrics, filters), F32)
    kernel = jnp.zeros((metrics, LANES), F32)
    for tap in range(TAPS):
        rows = pl.ds(tap * metrics, metrics)
        weighted = terms_ref[0, rows, :] * pool_a + terms_ref[1, rows, :] * pool_v
        mixing = mixing + dw_ref[:, tap : tap + 1] * weighted
        column = jnp.sum(pw_turned * weighted, 1, keepdims=True)
        kernel = kernel + jnp.where(lanes == tap, column, 0.0)
    mixing = mixing.T
    parts = sums_ref.shape[0]
    mix_rows, tap_rows = filters // parts, metrics // parts
    for part in range(parts):
        sums_ref[part, 0:mix_rows, :] = mixing[part * mix_rows : (part + 1) * mix_rows, :]
        sums_ref[part, mix_rows : mix_rows + tap_rows, :] = kernel[
            part * tap_rows : (part + 1) * tap_rows, :
        ]


def middle(own, pooled, partners, proj_weight, dw_weight, pw_turned, terms, parts, length):
    filters, width = proj_weight.shape
    metrics = pw_turned.shape[0]
    count = pooled.shape[0]
    whole = pl.BlockSpec(memory_space=pltpu.VMEM)
    rows = filters // parts + metrics // parts
    return pl.pallas_call(
        functools.partial(middle_kernel, length),
        in_specs=[pl.BlockSpec(memory_space=pltpu.SMEM)] + [whole] * 6,
        out_specs=[whole] * 4,
        out_shape=[
            jax.ShapeDtypeStruct((count, 1), F32),
            jax.ShapeDtypeStruct((count, width), BF16),
            jax.ShapeDtypeStruct((count, width), BF16),
            jax.ShapeDtypeStruct((parts, rows, metrics), F32),
        ],
        scratch_shapes=[pltpu.VMEM((count, width), F32), pltpu.VMEM((count, width), F32)],
        compiler_params=pltpu.CompilerParams(vmem_limit_bytes=24 << 20),
    )(own, pooled, partners, proj_weight, dw_weight, pw_turned, terms)


def swap(value, axis):
    return lax.all_to_all(value, axis, 0, 0, tiled=True)


def fold_kernel(parts_ref, out_ref):
    out_ref[...] = jnp.broadcast_to(jnp.sum(parts_ref[...], 0)[None], out_ref.shape)


def fold(parts, copies):
    whole = pl.BlockSpec(memory_space=pltpu.VMEM)
    return pl.pallas_call(
        fold_kernel,
        in_specs=[whole],
        out_specs=whole,
        out_shape=jax.ShapeDtypeStruct((copies,) + parts.shape[1:], F32),
        compiler_params=pltpu.CompilerParams(vmem_limit_bytes=4 << 20),
    )(parts)


def unpack_kernel(index_ref, shares_ref, mix_ref, tap_ref):
    parts, rows, width = shares_ref.shape
    mix_rows = mix_ref.shape[0] // parts
    for part in range(parts):
        mix_ref[part * mix_rows : (part + 1) * mix_rows, :] = shares_ref[part, 0:mix_rows, :]
    taps = shares_ref[index_ref[0], mix_rows:rows, :]
    tap_ref[...] = taps.T[0 : tap_ref.shape[0], :]


def unpack(chan_index, shares, mix_rows):
    parts, rows, width = shares.shape
    whole = pl.BlockSpec(memory_space=pltpu.VMEM)
    return pl.pallas_call(
        unpack_kernel,
        in_specs=[pl.BlockSpec(memory_space=pltpu.SMEM), whole],
        out_specs=[whole, whole],
        out_shape=[
            jax.ShapeDtypeStruct((parts * mix_rows, width), F32),
            jax.ShapeDtypeStruct((TAPS, rows - mix_rows), F32),
        ],
        compiler_params=pltpu.CompilerParams(vmem_limit_bytes=4 << 20),
    )(chan_index.astype(jnp.int32).reshape(1), shares)


def body(anchors, views, dw_weight, pw_weight, proj_weight, partner):
    chan_index = lax.axis_index("chan")
    dp_index = lax.axis_index("dp")
    chan_count = lax.axis_size("chan")
    dp_count = lax.axis_size("dp")
    pairs, local_metrics, length = anchors.shape
    filters, metrics = pw_weight.shape
    width = proj_weight.shape[1]
    dw_turned, pw_turned = dw_weight.T, pw_weight.T

    partners = lax.dynamic_update_slice_in_dim(
        jnp.zeros((dp_count, pairs), jnp.int32), partner[None], dp_index, 0
    )
    bit = 1
    while bit < dp_count:
        partners += lax.ppermute(partners, "dp", [(i, i ^ bit) for i in range(dp_count)])
        bit *= 2
    partners = partners.reshape(pairs * dp_count, 1)
    traces = swap(jnp.stack([anchors, views], 1), "chan")
    traces, partners = lax.optimization_barrier((traces, partners))
    message = pool_pass(traces, dw_turned, pw_turned, dp_count * chan_count)
    pooled = swap(message, ("dp", "chan")).reshape(message.shape[0], -1)
    terms = terms_pass(traces, dw_turned, pw_turned)
    own = (dp_index * chan_count + chan_index).astype(jnp.int32).reshape(1)
    losses, grad_a, grad_v, sums = middle(
        own, pooled, partners, proj_weight, dw_weight, pw_turned, terms, dp_count, length
    )

    shares = fold(swap(sums, "dp"), chan_count)
    shares = fold(swap(shares, "chan"), dp_count)
    grad_pw, grad_dw = unpack(chan_index, swap(shares, "dp"), filters // dp_count)

    cols = width // dp_count
    rows = filters // chan_count

    def proj_part(offset, grad):
        features = lax.dynamic_slice_in_dim(pooled, offset + chan_index * rows, rows, 1)
        part = lax.dynamic_slice_in_dim(grad, dp_index * cols, cols, 1)
        return lax.dot_general(
            features, part, (((0,), (0,)), ((), ())), preferred_element_type=F32
        )

    grad_proj = proj_part(0, grad_a) + proj_part(filters, grad_v)
    loss = lax.dynamic_slice_in_dim(losses, dp_index * pairs, pairs, 0).reshape(pairs)
    return (loss, grad_dw.T, grad_pw, grad_proj)


def solution(mesh):
    placed = (P("dp", "chan", None), P("dp", "chan", None), P(), P(), P(), P("dp"))
    return jax.shard_map(
        body,
        mesh=mesh,
        in_specs=placed,
        out_specs=(P("dp"), P("chan", None), P(), P("chan", "dp")),
        check_vma=False,
    )
```

```python
import functools

import jax
import jax.numpy as jnp
from jax import lax
from jax.experimental import pallas as pl
from jax.experimental.pallas import tpu as pltpu
from jax.sharding import PartitionSpec as P

TAPS = 4
TAP_SPACING = 16
RIM = (TAPS - 1) * TAP_SPACING
LOGIT_SCALE = 16.0
LANES = 128
SUBLANES = 8
BLOCK = 256
F32 = jnp.float32
BF16 = jnp.bfloat16


def mixed_half(flipped, begin, dw_turned_ref, half, turned):
    steps = flipped.shape[0]
    turned[RIM + begin : RIM + begin + steps, :] = flipped
    running = dw_turned_ref[0:1, :] * flipped
    for tap in range(1, TAPS):
        first = RIM + begin - tap * TAP_SPACING
        running = running + dw_turned_ref[tap : tap + 1, :] * turned[first : first + steps, :]
    return lax.dot_general(
        running.astype(BF16), half, (((1,), (1,)), ((), ())), preferred_element_type=F32
    )


def pool_kernel(x_ref, dw_turned_ref, pw_ref, message_ref, turned):
    sources, pair, local, length = x_ref.shape
    filters = pw_ref.shape[0]
    half = pw_ref[...] * 0.5
    rows = []
    for trace in range(pair):
        held = turned.at[trace]
        held[0:RIM, :] = jnp.zeros((RIM, sources * local), F32)
        total = jnp.zeros((SUBLANES, filters), F32)
        for begin in range(0, length, BLOCK):
            block = x_ref[:, trace, :, begin : begin + BLOCK]
            flipped = block.reshape(sources * local, BLOCK).T.astype(F32)
            value = mixed_half(flipped, begin, dw_turned_ref, half, held)
            silu = value + value * jnp.tanh(value)
            total = total + jnp.sum(silu.reshape(BLOCK // SUBLANES, SUBLANES, filters), 0)
        rows.append(jnp.sum(total, 0, keepdims=True) / length)
    rows = jnp.concatenate(rows, 0).astype(BF16)
    message_ref[...] = jnp.broadcast_to(rows[None], message_ref.shape)


def pool_pass(traces, dw_turned, pw_weight, devices):
    sources, pair, local, length = traces.shape
    filters, metrics = pw_weight.shape
    whole = pl.BlockSpec(memory_space=pltpu.VMEM)
    return pl.pallas_call(
        pool_kernel,
        in_specs=[whole] * 3,
        out_specs=whole,
        out_shape=jax.ShapeDtypeStruct((devices, pair, filters), BF16),
        scratch_shapes=[pltpu.VMEM((pair, length + RIM, metrics), F32)],
        compiler_params=pltpu.CompilerParams(vmem_limit_bytes=12 << 20),
    )(traces, dw_turned, pw_weight)


def terms_kernel(x_ref, dw_turned_ref, pw_ref, terms_ref, turned, slope, plain):
    sources, pair, local, length = x_ref.shape
    metrics = sources * local
    half = pw_ref[...] * 0.5
    for trace in range(pair):
        held = turned.at[trace]
        bends = slope.at[trace]
        flat = plain.at[trace]
        held[0:RIM, :] = jnp.zeros((RIM, metrics), F32)
        bends[length : length + RIM, :] = jnp.zeros((RIM, bends.shape[1]), BF16)
        for begin in range(0, length, BLOCK):
            block = x_ref[:, trace, :, begin : begin + BLOCK].reshape(metrics, BLOCK)
            flat[:, begin : begin + BLOCK] = block
            value = mixed_half(block.T.astype(F32), begin, dw_turned_ref, half, held)
            bent = jnp.tanh(value)
            bends[begin : begin + BLOCK, :] = (
                (1.0 + bent) * (1.0 + value * (1.0 - bent))
            ).astype(BF16)
        for tap in range(TAPS):
            first = tap * TAP_SPACING
            terms_ref[trace, tap * metrics : (tap + 1) * metrics, :] = jnp.dot(
                flat[...], bends[first : first + length, :], preferred_element_type=F32
            )


def terms_pass(traces, dw_turned, pw_weight):
    sources, pair, local, length = traces.shape
    filters, metrics = pw_weight.shape
    whole = pl.BlockSpec(memory_space=pltpu.VMEM)
    return pl.pallas_call(
        terms_kernel,
        in_specs=[whole] * 3,
        out_specs=whole,
        out_shape=jax.ShapeDtypeStruct((pair, metrics * TAPS, filters), F32),
        scratch_shapes=[
            pltpu.VMEM((pair, length + RIM, metrics), F32),
            pltpu.VMEM((pair, length + RIM, filters), BF16),
            pltpu.VMEM((pair, metrics, length), BF16),
        ],
        compiler_params=pltpu.CompilerParams(vmem_limit_bytes=24 << 20),
    )(traces, dw_turned, pw_weight)


def middle_kernel(
    length, own_ref, pooled_ref, partner_ref, proj_ref, dw_ref, pw_turned_ref, terms_ref,
    loss_ref, grad_a_ref, grad_v_ref, sums_ref, held_a, held_v,
):
    filters, width = proj_ref.shape
    count = pooled_ref.shape[0]
    metrics = pw_turned_ref.shape[0]
    factor = LOGIT_SCALE / width
    proj = proj_ref[...]

    def normed(pooled):
        embedding = jnp.dot(pooled, proj, preferred_element_type=F32)
        inverse = lax.rsqrt(jnp.mean(embedding * embedding, 1, keepdims=True) + 1e-06)
        return embedding * inverse, inverse

    unit_a, inverse_a = normed(pooled_ref[:, 0:filters])
    unit_v, inverse_v = normed(pooled_ref[:, filters : 2 * filters])
    queries = unit_a.astype(BF16)
    keys = unit_v.astype(BF16)
    logits = factor * lax.dot_general(
        queries, keys, (((1,), (1,)), ((), ())), preferred_element_type=F32
    )
    columns = lax.broadcasted_iota(jnp.int32, (count, count), 1)
    matches = columns == partner_ref[...]
    weights = jnp.exp(logits - LOGIT_SCALE)
    totals = jnp.sum(weights, 1, keepdims=True)
    positive = jnp.sum(jnp.where(matches, logits, 0.0), 1, keepdims=True)
    loss_ref[...] = LOGIT_SCALE + jnp.log(totals) - positive
    coeffs = (weights / totals - jnp.where(matches, 1.0, 0.0)).astype(BF16)
    unit_grad_a = factor * jnp.dot(coeffs, keys, preferred_element_type=F32)
    unit_grad_v = factor * lax.dot_general(
        coeffs, queries, (((0,), (0,)), ((), ())), preferred_element_type=F32
    )
    own = own_ref[0]

    def pool_grad(unit, inverse, unit_grad, out_ref, held):
        grad = inverse * (unit_grad - unit * jnp.mean(unit * unit_grad, 1, keepdims=True))
        grad = grad.astype(BF16)
        out_ref[...] = grad
        held[...] = grad.astype(F32)
        row = jnp.broadcast_to(held[pl.ds(own, 1), :], (16, width)).astype(BF16)
        pool = lax.dot_general(row, proj, (((1,), (1,)), ((), ())), preferred_element_type=F32)
        return pool[0:1, :] * (0.5 / length)

    pool_a = pool_grad(unit_a, inverse_a, unit_grad_a, grad_a_ref, held_a)
    pool_v = pool_grad(unit_v, inverse_v, unit_grad_v, grad_v_ref, held_v)

    pw_turned = pw_turned_ref[...].astype(F32)
    lanes = lax.broadcasted_iota(jnp.int32, (metrics, LANES), 1)
    mixing = jnp.zeros((metrics, filters), F32)
    kernel = jnp.zeros((metrics, LANES), F32)
    for tap in range(TAPS):
        rows = pl.ds(tap * metrics, metrics)
        weighted = terms_ref[0, rows, :] * pool_a + terms_ref[1, rows, :] * pool_v
        mixing = mixing + dw_ref[:, tap : tap + 1] * weighted
        column = jnp.sum(pw_turned * weighted, 1, keepdims=True)
        kernel = kernel + jnp.where(lanes == tap, column, 0.0)
    mixing = mixing.T
    kernel = kernel.T
    parts = sums_ref.shape[0]
    mix_rows = filters // parts
    for part in range(parts):
        for row in range(mix_rows):
            sums_ref[part, 0:1, row * LANES : (row + 1) * LANES] = mixing[
                part * mix_rows + row : part * mix_rows + row + 1, :
            ]
        sums_ref[part, 0:1, mix_rows * LANES :] = kernel[part : part + 1, :]


def middle(own, pooled, partners, proj_weight, dw_weight, pw_turned, terms, parts, length):
    filters, width = proj_weight.shape
    metrics = pw_turned.shape[0]
    count = pooled.shape[0]
    whole = pl.BlockSpec(memory_space=pltpu.VMEM)
    packed = (filters // parts + 1) * metrics
    return pl.pallas_call(
        functools.partial(middle_kernel, length),
        in_specs=[pl.BlockSpec(memory_space=pltpu.SMEM)] + [whole] * 6,
        out_specs=[whole] * 4,
        out_shape=[
            jax.ShapeDtypeStruct((count, 1), F32),
            jax.ShapeDtypeStruct((count, width), BF16),
            jax.ShapeDtypeStruct((count, width), BF16),
            jax.ShapeDtypeStruct((parts, 1, packed), F32),
        ],
        scratch_shapes=[pltpu.VMEM((count, width), F32), pltpu.VMEM((count, width), F32)],
        compiler_params=pltpu.CompilerParams(vmem_limit_bytes=24 << 20),
    )(own, pooled, partners, proj_weight, dw_weight, pw_turned, terms)


def swap(value, axis):
    return lax.all_to_all(value, axis, 0, 0, tiled=True)


def fold_kernel(parts_ref, out_ref):
    out_ref[...] = jnp.broadcast_to(jnp.sum(parts_ref[...], 0)[None], out_ref.shape)


def fold(parts, copies):
    whole = pl.BlockSpec(memory_space=pltpu.VMEM)
    return pl.pallas_call(
        fold_kernel,
        in_specs=[whole],
        out_specs=whole,
        out_shape=jax.ShapeDtypeStruct((copies,) + parts.shape[1:], F32),
        compiler_params=pltpu.CompilerParams(vmem_limit_bytes=4 << 20),
    )(parts)


def unpack_kernel(index_ref, shares_ref, mix_ref, tap_ref):
    parts = shares_ref.shape[0]
    mix_rows = mix_ref.shape[0] // parts
    taps, local = tap_ref.shape
    for part in range(parts):
        for row in range(mix_rows):
            mix_ref[part * mix_rows + row : part * mix_rows + row + 1, :] = shares_ref[
                part, 0:1, row * LANES : (row + 1) * LANES
            ]
    back = lax.rem(LANES - index_ref[0] * local, LANES)
    rows = jnp.concatenate(
        [shares_ref[tap, 0:1, mix_rows * LANES :] for tap in range(taps)] * (SUBLANES // taps), 0
    )
    tap_ref[...] = pltpu.roll(rows, back, 1)[0:taps, 0:local]


def unpack(chan_index, shares, filters, local_metrics):
    whole = pl.BlockSpec(memory_space=pltpu.VMEM)
    return pl.pallas_call(
        unpack_kernel,
        in_specs=[pl.BlockSpec(memory_space=pltpu.SMEM), whole],
        out_specs=[whole, whole],
        out_shape=[
            jax.ShapeDtypeStruct((filters, LANES), F32),
            jax.ShapeDtypeStruct((TAPS, local_metrics), F32),
        ],
        compiler_params=pltpu.CompilerParams(vmem_limit_bytes=4 << 20),
    )(chan_index.astype(jnp.int32).reshape(1), shares)


def body(anchors, views, dw_weight, pw_weight, proj_weight, partner):
    chan_index = lax.axis_index("chan")
    dp_index = lax.axis_index("dp")
    chan_count = lax.axis_size("chan")
    dp_count = lax.axis_size("dp")
    pairs, local_metrics, length = anchors.shape
    filters, metrics = pw_weight.shape
    width = proj_weight.shape[1]
    dw_turned = dw_weight.T

    traces = swap(jnp.stack([anchors, views], 1), "chan")
    message = pool_pass(traces, dw_turned, pw_weight, dp_count * chan_count)
    message, partner, pw_later = lax.optimization_barrier((message, partner, pw_weight))
    partners = lax.dynamic_update_slice_in_dim(
        jnp.zeros((dp_count, pairs), jnp.int32), partner[None], dp_index, 0
    )
    bit = 1
    while bit < dp_count:
        partners += lax.ppermute(partners, "dp", [(i, i ^ bit) for i in range(dp_count)])
        bit *= 2
    partners = partners.reshape(pairs * dp_count, 1)
    pooled = swap(message, ("dp", "chan")).reshape(message.shape[0], -1)
    terms = terms_pass(traces, dw_turned, pw_weight)
    own = (dp_index * chan_count + chan_index).astype(jnp.int32).reshape(1)
    losses, grad_a, grad_v, sums = middle(
        own, pooled, partners, proj_weight, dw_weight, pw_later.T, terms, dp_count, length
    )

    shares = fold(swap(sums, "dp"), chan_count)
    shares = fold(swap(shares, "chan"), dp_count)
    grad_pw, grad_dw = unpack(chan_index, swap(shares, "dp"), filters, local_metrics)

    cols = width // dp_count
    rows = filters // chan_count

    def proj_part(offset, grad):
        features = lax.dynamic_slice_in_dim(pooled, offset + chan_index * rows, rows, 1)
        part = lax.dynamic_slice_in_dim(grad, dp_index * cols, cols, 1)
        return lax.dot_general(
            features, part, (((0,), (0,)), ((), ())), preferred_element_type=F32
        )

    grad_proj = proj_part(0, grad_a) + proj_part(filters, grad_v)
    loss = lax.dynamic_slice_in_dim(losses, dp_index * pairs, pairs, 0).reshape(pairs)
    return (loss, grad_dw.T, grad_pw, grad_proj)


def solution(mesh):
    placed = (P("dp", "chan", None), P("dp", "chan", None), P(), P(), P(), P("dp"))
    return jax.shard_map(
        body,
        mesh=mesh,
        in_specs=placed,
        out_specs=(P("dp"), P("chan", None), P(), P("chan", "dp")),
        check_vma=False,
    )
```

```python
import functools

import jax
import jax.numpy as jnp
from jax import lax
from jax.experimental import pallas as pl
from jax.experimental.pallas import tpu as pltpu
from jax.sharding import PartitionSpec as P

TAPS = 4
TAP_SPACING = 16
RIM = (TAPS - 1) * TAP_SPACING
LOGIT_SCALE = 16.0
LANES = 128
SUBLANES = 8
BLOCK = 256
F32 = jnp.float32
BF16 = jnp.bfloat16


def mixed_half(flipped, begin, dw_turned_ref, half, turned):
    steps = flipped.shape[0]
    turned[RIM + begin : RIM + begin + steps, :] = flipped
    running = dw_turned_ref[0:1, :] * flipped
    for tap in range(1, TAPS):
        first = RIM + begin - tap * TAP_SPACING
        running = running + dw_turned_ref[tap : tap + 1, :] * turned[first : first + steps, :]
    return jnp.dot(running.astype(BF16), half, preferred_element_type=F32)


def pool_kernel(x_ref, dw_turned_ref, pw_turned_ref, message_ref, turned):
    sources, pair, local, length = x_ref.shape
    filters = pw_turned_ref.shape[1]
    half = pw_turned_ref[...] * 0.5
    rows = []
    for trace in range(pair):
        held = turned
        held[0:RIM, :] = jnp.zeros((RIM, sources * local), F32)
        total = jnp.zeros((SUBLANES, filters), F32)
        for begin in range(0, length, BLOCK):
            block = x_ref[:, trace, :, begin : begin + BLOCK]
            flipped = block.reshape(sources * local, BLOCK).T.astype(F32)
            value = mixed_half(flipped, begin, dw_turned_ref, half, held)
            silu = value + value * jnp.tanh(value)
            total = total + jnp.sum(silu.reshape(BLOCK // SUBLANES, SUBLANES, filters), 0)
        rows.append(jnp.sum(total, 0, keepdims=True) / length)
    rows = jnp.concatenate(rows, 0).astype(BF16)
    message_ref[...] = jnp.broadcast_to(rows[None], message_ref.shape)


def pool_pass(traces, dw_turned, pw_turned, devices):
    sources, pair, local, length = traces.shape
    metrics, filters = pw_turned.shape
    whole = pl.BlockSpec(memory_space=pltpu.VMEM)
    return pl.pallas_call(
        pool_kernel,
        in_specs=[whole] * 3,
        out_specs=whole,
        out_shape=jax.ShapeDtypeStruct((devices, pair, filters), BF16),
        scratch_shapes=[pltpu.VMEM((length + RIM, metrics), F32)],
        compiler_params=pltpu.CompilerParams(vmem_limit_bytes=8 << 20),
    )(traces, dw_turned, pw_turned)


def terms_kernel(x_ref, dw_turned_ref, pw_turned_ref, terms_ref, turned, slope, plain):
    sources, pair, local, length = x_ref.shape
    metrics = sources * local
    half = pw_turned_ref[...] * 0.5
    for trace in range(pair):
        held, bends, flat = turned, slope, plain
        held[0:RIM, :] = jnp.zeros((RIM, metrics), F32)
        bends[length : length + RIM, :] = jnp.zeros((RIM, bends.shape[1]), BF16)
        for begin in range(0, length, BLOCK):
            block = x_ref[:, trace, :, begin : begin + BLOCK].reshape(metrics, BLOCK)
            flat[:, begin : begin + BLOCK] = block
            value = mixed_half(block.T.astype(F32), begin, dw_turned_ref, half, held)
            bent = jnp.tanh(value)
            bends[begin : begin + BLOCK, :] = (
                (1.0 + bent) * (1.0 + value * (1.0 - bent))
            ).astype(BF16)
        for tap in range(TAPS):
            first = tap * TAP_SPACING
            terms_ref[trace, tap * metrics : (tap + 1) * metrics, :] = jnp.dot(
                flat[...], bends[first : first + length, :], preferred_element_type=F32
            )


def terms_pass(traces, dw_turned, pw_turned):
    sources, pair, local, length = traces.shape
    metrics, filters = pw_turned.shape
    whole = pl.BlockSpec(memory_space=pltpu.VMEM)
    return pl.pallas_call(
        terms_kernel,
        in_specs=[whole] * 3,
        out_specs=whole,
        out_shape=jax.ShapeDtypeStruct((pair, metrics * TAPS, filters), F32),
        scratch_shapes=[
            pltpu.VMEM((length + RIM, metrics), F32),
            pltpu.VMEM((length + RIM, filters), BF16),
            pltpu.VMEM((metrics, length), BF16),
        ],
        compiler_params=pltpu.CompilerParams(vmem_limit_bytes=12 << 20),
    )(traces, dw_turned, pw_turned)


def middle_kernel(
    length, own_ref, pooled_ref, partner_ref, proj_ref, dw_ref, pw_turned_ref, terms_ref,
    loss_ref, grad_a_ref, grad_v_ref, sums_ref, held_a, held_v,
):
    filters, width = proj_ref.shape
    count = pooled_ref.shape[0]
    metrics = pw_turned_ref.shape[0]
    factor = LOGIT_SCALE / width
    proj = proj_ref[...]

    def normed(pooled):
        embedding = jnp.dot(pooled, proj, preferred_element_type=F32)
        inverse = lax.rsqrt(jnp.mean(embedding * embedding, 1, keepdims=True) + 1e-06)
        return embedding * inverse, inverse

    unit_a, inverse_a = normed(pooled_ref[:, 0:filters])
    unit_v, inverse_v = normed(pooled_ref[:, filters : 2 * filters])
    queries = unit_a.astype(BF16)
    keys = unit_v.astype(BF16)
    logits = factor * lax.dot_general(
        queries, keys, (((1,), (1,)), ((), ())), preferred_element_type=F32
    )
    columns = lax.broadcasted_iota(jnp.int32, (count, count), 1)
    matches = columns == partner_ref[...]
    weights = jnp.exp(logits - LOGIT_SCALE)
    totals = jnp.sum(weights, 1, keepdims=True)
    positive = jnp.sum(jnp.where(matches, logits, 0.0), 1, keepdims=True)
    loss_ref[...] = LOGIT_SCALE + jnp.log(totals) - positive
    coeffs = (weights / totals - jnp.where(matches, 1.0, 0.0)).astype(BF16)
    unit_grad_a = factor * jnp.dot(coeffs, keys, preferred_element_type=F32)
    unit_grad_v = factor * lax.dot_general(
        coeffs, queries, (((0,), (0,)), ((), ())), preferred_element_type=F32
    )
    own = own_ref[0]

    def pool_grad(unit, inverse, unit_grad, out_ref, held):
        grad = inverse * (unit_grad - unit * jnp.mean(unit * unit_grad, 1, keepdims=True))
        grad = grad.astype(BF16)
        out_ref[...] = grad
        held[...] = grad.astype(F32)
        row = jnp.broadcast_to(held[pl.ds(own, 1), :], (16, width)).astype(BF16)
        pool = lax.dot_general(row, proj, (((1,), (1,)), ((), ())), preferred_element_type=F32)
        return pool[0:1, :] * (0.5 / length)

    pool_a = pool_grad(unit_a, inverse_a, unit_grad_a, grad_a_ref, held_a)
    pool_v = pool_grad(unit_v, inverse_v, unit_grad_v, grad_v_ref, held_v)

    pw_turned = pw_turned_ref[...].astype(F32)
    lanes = lax.broadcasted_iota(jnp.int32, (metrics, LANES), 1)
    mixing = jnp.zeros((metrics, filters), F32)
    kernel = jnp.zeros((metrics, LANES), F32)
    for tap in range(TAPS):
        rows = pl.ds(tap * metrics, metrics)
        weighted = terms_ref[0, rows, :] * pool_a + terms_ref[1, rows, :] * pool_v
        mixing = mixing + dw_ref[:, tap : tap + 1] * weighted
        column = jnp.sum(pw_turned * weighted, 1, keepdims=True)
        kernel = kernel + jnp.where(lanes == tap, column, 0.0)
    mixing = mixing.T
    kernel = kernel.T
    parts = sums_ref.shape[0]
    mix_rows = filters // parts
    for part in range(parts):
        for row in range(mix_rows):
            sums_ref[part, 0:1, row * LANES : (row + 1) * LANES] = mixing[
                part * mix_rows + row : part * mix_rows + row + 1, :
            ]
        sums_ref[part, 0:1, mix_rows * LANES :] = kernel[part : part + 1, :]


def middle(own, pooled, partners, proj_weight, dw_weight, pw_turned, terms, parts, length):
    filters, width = proj_weight.shape
    metrics = pw_turned.shape[0]
    count = pooled.shape[0]
    whole = pl.BlockSpec(memory_space=pltpu.VMEM)
    packed = (filters // parts + 1) * metrics
    return pl.pallas_call(
        functools.partial(middle_kernel, length),
        in_specs=[pl.BlockSpec(memory_space=pltpu.SMEM)] + [whole] * 6,
        out_specs=[whole] * 4,
        out_shape=[
            jax.ShapeDtypeStruct((count, 1), F32),
            jax.ShapeDtypeStruct((count, width), BF16),
            jax.ShapeDtypeStruct((count, width), BF16),
            jax.ShapeDtypeStruct((parts, 1, packed), F32),
        ],
        scratch_shapes=[pltpu.VMEM((count, width), F32), pltpu.VMEM((count, width), F32)],
        compiler_params=pltpu.CompilerParams(vmem_limit_bytes=24 << 20),
    )(own, pooled, partners, proj_weight, dw_weight, pw_turned, terms)


def swap(value, axis):
    return lax.all_to_all(value, axis, 0, 0, tiled=True)


def fold_kernel(parts_ref, out_ref):
    out_ref[...] = jnp.broadcast_to(jnp.sum(parts_ref[...], 0)[None], out_ref.shape)


def fold(parts, copies):
    whole = pl.BlockSpec(memory_space=pltpu.VMEM)
    return pl.pallas_call(
        fold_kernel,
        in_specs=[whole],
        out_specs=whole,
        out_shape=jax.ShapeDtypeStruct((copies,) + parts.shape[1:], F32),
        compiler_params=pltpu.CompilerParams(vmem_limit_bytes=4 << 20),
    )(parts)


def unpack_kernel(index_ref, shares_ref, mix_ref, tap_ref):
    parts = shares_ref.shape[0]
    mix_rows = mix_ref.shape[0] // parts
    taps, local = tap_ref.shape
    for part in range(parts):
        for row in range(mix_rows):
            mix_ref[part * mix_rows + row : part * mix_rows + row + 1, :] = shares_ref[
                part, 0:1, row * LANES : (row + 1) * LANES
            ]
    back = lax.rem(LANES - index_ref[0] * local, LANES)
    rows = jnp.concatenate(
        [shares_ref[tap, 0:1, mix_rows * LANES :] for tap in range(taps)] * (SUBLANES // taps), 0
    )
    tap_ref[...] = pltpu.roll(rows, back, 1)[0:taps, 0:local]


def unpack(chan_index, shares, filters, local_metrics):
    whole = pl.BlockSpec(memory_space=pltpu.VMEM)
    return pl.pallas_call(
        unpack_kernel,
        in_specs=[pl.BlockSpec(memory_space=pltpu.SMEM), whole],
        out_specs=[whole, whole],
        out_shape=[
            jax.ShapeDtypeStruct((filters, LANES), F32),
            jax.ShapeDtypeStruct((TAPS, local_metrics), F32),
        ],
        compiler_params=pltpu.CompilerParams(vmem_limit_bytes=4 << 20),
    )(chan_index.astype(jnp.int32).reshape(1), shares)


def body(anchors, views, dw_weight, pw_weight, proj_weight, partner):
    chan_index = lax.axis_index("chan")
    dp_index = lax.axis_index("dp")
    chan_count = lax.axis_size("chan")
    dp_count = lax.axis_size("dp")
    pairs, local_metrics, length = anchors.shape
    filters, metrics = pw_weight.shape
    width = proj_weight.shape[1]
    dw_turned, pw_turned = dw_weight.T, pw_weight.T

    partners = lax.dynamic_update_slice_in_dim(
        jnp.zeros((dp_count, pairs), jnp.int32), partner[None], dp_index, 0
    )
    bit = 1
    while bit < dp_count:
        partners += lax.ppermute(partners, "dp", [(i, i ^ bit) for i in range(dp_count)])
        bit *= 2
    partners = partners.reshape(pairs * dp_count, 1)
    traces = swap(jnp.stack([anchors, views], 1), "chan")
    traces, partners = lax.optimization_barrier((traces, partners))
    message = pool_pass(traces, dw_turned, pw_turned, dp_count * chan_count)
    pooled = swap(message, ("dp", "chan")).reshape(message.shape[0], -1)
    terms = terms_pass(traces, dw_turned, pw_turned)
    own = (dp_index * chan_count + chan_index).astype(jnp.int32).reshape(1)
    losses, grad_a, grad_v, sums = middle(
        own, pooled, partners, proj_weight, dw_weight, pw_turned, terms, dp_count, length
    )

    shares = fold(swap(sums, "dp"), chan_count)
    shares = fold(swap(shares, "chan"), dp_count)
    grad_pw, grad_dw = unpack(chan_index, swap(shares, "dp"), filters, local_metrics)

    cols = width // dp_count
    rows = filters // chan_count

    def proj_part(offset, grad):
        features = lax.dynamic_slice_in_dim(pooled, offset + chan_index * rows, rows, 1)
        part = lax.dynamic_slice_in_dim(grad, dp_index * cols, cols, 1)
        return lax.dot_general(
            features, part, (((0,), (0,)), ((), ())), preferred_element_type=F32
        )

    grad_proj = proj_part(0, grad_a) + proj_part(filters, grad_v)
    loss = lax.dynamic_slice_in_dim(losses, dp_index * pairs, pairs, 0).reshape(pairs)
    return (loss, grad_dw.T, grad_pw, grad_proj)


def solution(mesh):
    placed = (P("dp", "chan", None), P("dp", "chan", None), P(), P(), P(), P("dp"))
    return jax.shard_map(
        body,
        mesh=mesh,
        in_specs=placed,
        out_specs=(P("dp"), P("chan", None), P(), P("chan", "dp")),
        check_vma=False,
    )
```

```python
import functools

import jax
import jax.numpy as jnp
from jax import lax
from jax.experimental import pallas as pl
from jax.experimental.pallas import tpu as pltpu
from jax.sharding import PartitionSpec as P

TAPS = 4
TAP_SPACING = 16
RIM = (TAPS - 1) * TAP_SPACING
LOGIT_SCALE = 16.0
LANES = 128
SUBLANES = 8
BLOCK = 256
F32 = jnp.float32
BF16 = jnp.bfloat16


def mixed_half(flipped, begin, dw_turned_ref, half, turned):
    steps = flipped.shape[0]
    turned[RIM + begin : RIM + begin + steps, :] = flipped
    running = dw_turned_ref[0:1, :] * flipped
    for tap in range(1, TAPS):
        first = RIM + begin - tap * TAP_SPACING
        running = running + dw_turned_ref[tap : tap + 1, :] * turned[first : first + steps, :]
    return jnp.dot(running.astype(BF16), half, preferred_element_type=F32)


def pool_kernel(x_ref, dw_turned_ref, pw_turned_ref, message_ref, turned):
    sources, pair, local, length = x_ref.shape
    filters = pw_turned_ref.shape[1]
    half = pw_turned_ref[...] * 0.5
    rows = []
    for trace in range(pair):
        held = turned.at[trace]
        held[0:RIM, :] = jnp.zeros((RIM, sources * local), F32)
        total = jnp.zeros((SUBLANES, filters), F32)
        for begin in range(0, length, BLOCK):
            block = x_ref[:, trace, :, begin : begin + BLOCK]
            flipped = block.reshape(sources * local, BLOCK).T.astype(F32)
            value = mixed_half(flipped, begin, dw_turned_ref, half, held)
            silu = value + value * jnp.tanh(value)
            total = total + jnp.sum(silu.reshape(BLOCK // SUBLANES, SUBLANES, filters), 0)
        rows.append(jnp.sum(total, 0, keepdims=True) / length)
    rows = jnp.concatenate(rows, 0).astype(BF16)
    message_ref[...] = jnp.broadcast_to(rows[None], message_ref.shape)


def pool_pass(traces, dw_turned, pw_turned, devices):
    sources, pair, local, length = traces.shape
    metrics, filters = pw_turned.shape
    whole = pl.BlockSpec(memory_space=pltpu.VMEM)
    return pl.pallas_call(
        pool_kernel,
        in_specs=[whole] * 3,
        out_specs=whole,
        out_shape=jax.ShapeDtypeStruct((devices, pair, filters), BF16),
        scratch_shapes=[pltpu.VMEM((pair, length + RIM, metrics), F32)],
        compiler_params=pltpu.CompilerParams(vmem_limit_bytes=8 << 20),
    )(traces, dw_turned, pw_turned)


def terms_kernel(x_ref, dw_turned_ref, pw_turned_ref, terms_ref, turned, slope, plain):
    sources, pair, local, length = x_ref.shape
    metrics = sources * local
    half = pw_turned_ref[...] * 0.5
    for trace in range(pair):
        held, bends, flat = turned, slope, plain
        held[0:RIM, :] = jnp.zeros((RIM, metrics), F32)
        bends[length : length + RIM, :] = jnp.zeros((RIM, bends.shape[1]), BF16)
        for begin in range(0, length, BLOCK):
            block = x_ref[:, trace, :, begin : begin + BLOCK].reshape(metrics, BLOCK)
            flat[:, begin : begin + BLOCK] = block
            value = mixed_half(block.T.astype(F32), begin, dw_turned_ref, half, held)
            bent = jnp.tanh(value)
            bends[begin : begin + BLOCK, :] = (
                (1.0 + bent) * (1.0 + value * (1.0 - bent))
            ).astype(BF16)
        for tap in range(TAPS):
            first = tap * TAP_SPACING
            terms_ref[trace, tap * metrics : (tap + 1) * metrics, :] = jnp.dot(
                flat[...], bends[first : first + length, :], preferred_element_type=F32
            )


def terms_pass(traces, dw_turned, pw_turned):
    sources, pair, local, length = traces.shape
    metrics, filters = pw_turned.shape
    whole = pl.BlockSpec(memory_space=pltpu.VMEM)
    return pl.pallas_call(
        terms_kernel,
        in_specs=[whole] * 3,
        out_specs=whole,
        out_shape=jax.ShapeDtypeStruct((pair, metrics * TAPS, filters), F32),
        scratch_shapes=[
            pltpu.VMEM((length + RIM, metrics), F32),
            pltpu.VMEM((length + RIM, filters), BF16),
            pltpu.VMEM((metrics, length), BF16),
        ],
        compiler_params=pltpu.CompilerParams(vmem_limit_bytes=12 << 20),
    )(traces, dw_turned, pw_turned)


def normed(embedding):
    inverse = lax.rsqrt(jnp.mean(embedding * embedding, 1, keepdims=True) + 1e-06)
    return embedding * inverse, inverse


def scored(queries, keys, partner, factor):
    count = queries.shape[0]
    logits = factor * lax.dot_general(
        queries, keys, (((1,), (1,)), ((), ())), preferred_element_type=F32
    )
    columns = lax.broadcasted_iota(jnp.int32, (count, count), 1)
    matches = columns == partner
    weights = jnp.exp(logits - LOGIT_SCALE)
    totals = jnp.sum(weights, 1, keepdims=True)
    positive = jnp.sum(jnp.where(matches, logits, 0.0), 1, keepdims=True)
    loss = LOGIT_SCALE + jnp.log(totals) - positive
    return loss, (weights / totals - jnp.where(matches, 1.0, 0.0)).astype(BF16)


def embed_grad(unit, inverse, unit_grad):
    grad = inverse * (unit_grad - unit * jnp.mean(unit * unit_grad, 1, keepdims=True))
    return grad.astype(BF16)


def own_kernel(
    length, own_ref, pooled_ref, partner_ref, proj_ref, dw_ref, pw_turned_ref, terms_ref,
    loss_ref, sums_ref, embed_a, embed_v, coeff_rows, coeff_columns,
):
    filters, width = proj_ref.shape
    metrics = pw_turned_ref.shape[0]
    factor = LOGIT_SCALE / width
    proj = proj_ref[...]
    embed_a[...] = jnp.dot(pooled_ref[:, 0:filters], proj, preferred_element_type=F32)
    embed_v[...] = jnp.dot(pooled_ref[:, filters : 2 * filters], proj, preferred_element_type=F32)
    queries = normed(embed_a[...])[0].astype(BF16)
    keys = normed(embed_v[...])[0].astype(BF16)
    loss, coeffs = scored(queries, keys, partner_ref[...], factor)
    loss_ref[...] = loss
    coeff_rows[...] = coeffs.astype(F32)
    coeff_columns[...] = coeffs.astype(F32).T
    own = own_ref[0]

    def pool_grad(coeff, others, embed):
        row = jnp.broadcast_to(coeff[pl.ds(own, 1), :], (16, coeff.shape[1])).astype(BF16)
        unit_grad = factor * jnp.dot(row, others, preferred_element_type=F32)
        unit, inverse = normed(embed[pl.ds(own, 1), :])
        grad = embed_grad(unit, inverse, unit_grad)
        pool = lax.dot_general(grad, proj, (((1,), (1,)), ((), ())), preferred_element_type=F32)
        return pool[0:1, :] * (0.5 / length)

    pool_a = pool_grad(coeff_rows, keys, embed_a)
    pool_v = pool_grad(coeff_columns, queries, embed_v)

    pw_turned = pw_turned_ref[...].astype(F32)
    lanes = lax.broadcasted_iota(jnp.int32, (metrics, LANES), 1)
    mixing = jnp.zeros((metrics, filters), F32)
    kernel = jnp.zeros((metrics, LANES), F32)
    for tap in range(TAPS):
        rows = pl.ds(tap * metrics, metrics)
        weighted = terms_ref[0, rows, :] * pool_a + terms_ref[1, rows, :] * pool_v
        mixing = mixing + dw_ref[:, tap : tap + 1] * weighted
        column = jnp.sum(pw_turned * weighted, 1, keepdims=True)
        kernel = kernel + jnp.where(lanes == tap, column, 0.0)
    mixing = mixing.T
    kernel = kernel.T
    parts = sums_ref.shape[0]
    mix_rows = filters // parts
    for part in range(parts):
        for row in range(mix_rows):
            sums_ref[part, 0:1, row * LANES : (row + 1) * LANES] = mixing[
                part * mix_rows + row : part * mix_rows + row + 1, :
            ]
        sums_ref[part, 0:1, mix_rows * LANES :] = kernel[part : part + 1, :]


def own_pass(own, pooled, partners, proj_weight, dw_weight, pw_turned, terms, parts, length):
    filters, width = proj_weight.shape
    metrics = pw_turned.shape[0]
    count = pooled.shape[0]
    whole = pl.BlockSpec(memory_space=pltpu.VMEM)
    packed = (filters // parts + 1) * metrics
    return pl.pallas_call(
        functools.partial(own_kernel, length),
        in_specs=[pl.BlockSpec(memory_space=pltpu.SMEM)] + [whole] * 6,
        out_specs=[whole] * 2,
        out_shape=[
            jax.ShapeDtypeStruct((count, 1), F32),
            jax.ShapeDtypeStruct((parts, 1, packed), F32),
        ],
        scratch_shapes=[
            pltpu.VMEM((count, width), F32),
            pltpu.VMEM((count, width), F32),
            pltpu.VMEM((count, count), F32),
            pltpu.VMEM((count, count), F32),
        ],
        compiler_params=pltpu.CompilerParams(vmem_limit_bytes=20 << 20),
    )(own, pooled, partners, proj_weight, dw_weight, pw_turned, terms)


def embed_kernel(pooled_ref, partner_ref, proj_ref, grad_a_ref, grad_v_ref):
    filters, width = proj_ref.shape
    factor = LOGIT_SCALE / width
    proj = proj_ref[...]

    def embedded(pooled):
        return normed(jnp.dot(pooled, proj, preferred_element_type=F32))

    unit_a, inverse_a = embedded(pooled_ref[:, 0:filters])
    unit_v, inverse_v = embedded(pooled_ref[:, filters : 2 * filters])
    queries = unit_a.astype(BF16)
    keys = unit_v.astype(BF16)
    _, coeffs = scored(queries, keys, partner_ref[...], factor)
    unit_grad_a = factor * jnp.dot(coeffs, keys, preferred_element_type=F32)
    unit_grad_v = factor * lax.dot_general(
        coeffs, queries, (((0,), (0,)), ((), ())), preferred_element_type=F32
    )
    grad_a_ref[...] = embed_grad(unit_a, inverse_a, unit_grad_a)
    grad_v_ref[...] = embed_grad(unit_v, inverse_v, unit_grad_v)


def embed_pass(pooled, partners, proj_weight):
    whole = pl.BlockSpec(memory_space=pltpu.VMEM)
    shape = jax.ShapeDtypeStruct((pooled.shape[0], proj_weight.shape[1]), BF16)
    return pl.pallas_call(
        embed_kernel,
        in_specs=[whole] * 3,
        out_specs=[whole] * 2,
        out_shape=[shape, shape],
        compiler_params=pltpu.CompilerParams(vmem_limit_bytes=20 << 20),
    )(pooled, partners, proj_weight)


def swap(value, axis):
    return lax.all_to_all(value, axis, 0, 0, tiled=True)


def fold_kernel(parts_ref, out_ref):
    out_ref[...] = jnp.broadcast_to(jnp.sum(parts_ref[...], 0)[None], out_ref.shape)


def fold(parts, copies):
    whole = pl.BlockSpec(memory_space=pltpu.VMEM)
    return pl.pallas_call(
        fold_kernel,
        in_specs=[whole],
        out_specs=whole,
        out_shape=jax.ShapeDtypeStruct((copies,) + parts.shape[1:], F32),
        compiler_params=pltpu.CompilerParams(vmem_limit_bytes=4 << 20),
    )(parts)


def unpack_kernel(index_ref, shares_ref, mix_ref, tap_ref):
    parts = shares_ref.shape[0]
    mix_rows = mix_ref.shape[0] // parts
    taps, local = tap_ref.shape
    for part in range(parts):
        for row in range(mix_rows):
            mix_ref[part * mix_rows + row : part * mix_rows + row + 1, :] = shares_ref[
                part, 0:1, row * LANES : (row + 1) * LANES
            ]
    back = lax.rem(LANES - index_ref[0] * local, LANES)
    rows = jnp.concatenate(
        [shares_ref[tap, 0:1, mix_rows * LANES :] for tap in range(taps)] * (SUBLANES // taps), 0
    )
    tap_ref[...] = pltpu.roll(rows, back, 1)[0:taps, 0:local]


def unpack(chan_index, shares, filters, local_metrics):
    whole = pl.BlockSpec(memory_space=pltpu.VMEM)
    return pl.pallas_call(
        unpack_kernel,
        in_specs=[pl.BlockSpec(memory_space=pltpu.SMEM), whole],
        out_specs=[whole, whole],
        out_shape=[
            jax.ShapeDtypeStruct((filters, LANES), F32),
            jax.ShapeDtypeStruct((TAPS, local_metrics), F32),
        ],
        compiler_params=pltpu.CompilerParams(vmem_limit_bytes=4 << 20),
    )(chan_index.astype(jnp.int32).reshape(1), shares)


def body(anchors, views, dw_weight, pw_weight, proj_weight, partner):
    chan_index = lax.axis_index("chan")
    dp_index = lax.axis_index("dp")
    chan_count = lax.axis_size("chan")
    dp_count = lax.axis_size("dp")
    pairs, local_metrics, length = anchors.shape
    filters, metrics = pw_weight.shape
    width = proj_weight.shape[1]
    dw_turned, pw_turned = dw_weight.T, pw_weight.T

    partners = lax.dynamic_update_slice_in_dim(
        jnp.zeros((dp_count, pairs), jnp.int32), partner[None], dp_index, 0
    )
    bit = 1
    while bit < dp_count:
        partners += lax.ppermute(partners, "dp", [(i, i ^ bit) for i in range(dp_count)])
        bit *= 2
    partners = partners.reshape(pairs * dp_count, 1)
    traces = swap(jnp.stack([anchors, views], 1), "chan")
    traces, partners = lax.optimization_barrier((traces, partners))
    message = pool_pass(traces, dw_turned, pw_turned, dp_count * chan_count)
    pooled = swap(message, ("dp", "chan")).reshape(message.shape[0], -1)
    terms = terms_pass(traces, dw_turned, pw_turned)
    own = (dp_index * chan_count + chan_index).astype(jnp.int32).reshape(1)
    losses, sums = own_pass(
        own, pooled, partners, proj_weight, dw_weight, pw_turned, terms, dp_count, length
    )
    grad_a, grad_v = embed_pass(pooled, partners, proj_weight)

    shares = fold(swap(sums, "dp"), chan_count)
    shares = fold(swap(shares, "chan"), dp_count)
    grad_pw, grad_dw = unpack(chan_index, swap(shares, "dp"), filters, local_metrics)

    cols = width // dp_count
    rows = filters // chan_count

    def proj_part(offset, grad):
        features = lax.dynamic_slice_in_dim(pooled, offset + chan_index * rows, rows, 1)
        part = lax.dynamic_slice_in_dim(grad, dp_index * cols, cols, 1)
        return lax.dot_general(
            features, part, (((0,), (0,)), ((), ())), preferred_element_type=F32
        )

    grad_proj = proj_part(0, grad_a) + proj_part(filters, grad_v)
    loss = lax.dynamic_slice_in_dim(losses, dp_index * pairs, pairs, 0).reshape(pairs)
    return (loss, grad_dw.T, grad_pw, grad_proj)


def solution(mesh):
    placed = (P("dp", "chan", None), P("dp", "chan", None), P(), P(), P(), P("dp"))
    return jax.shard_map(
        body,
        mesh=mesh,
        in_specs=placed,
        out_specs=(P("dp"), P("chan", None), P(), P("chan", "dp")),
        check_vma=False,
    )
```

```python
import functools

import jax
import jax.numpy as jnp
from jax import lax
from jax.experimental import pallas as pl
from jax.experimental.pallas import tpu as pltpu
from jax.sharding import PartitionSpec as P

TAPS = 4
TAP_SPACING = 16
RIM = (TAPS - 1) * TAP_SPACING
LOGIT_SCALE = 16.0
LANES = 128
SUBLANES = 8
BLOCK = 256
F32 = jnp.float32
BF16 = jnp.bfloat16


def mixed_half(flipped, begin, dw_turned_ref, half, turned):
    steps = flipped.shape[0]
    turned[RIM + begin : RIM + begin + steps, :] = flipped
    running = dw_turned_ref[0:1, :] * flipped
    for tap in range(1, TAPS):
        first = RIM + begin - tap * TAP_SPACING
        running = running + dw_turned_ref[tap : tap + 1, :] * turned[first : first + steps, :]
    return jnp.dot(running.astype(BF16), half, preferred_element_type=F32)


def pool_kernel(x_ref, dw_turned_ref, pw_turned_ref, message_ref, turned):
    sources, pair, local, length = x_ref.shape
    filters = pw_turned_ref.shape[1]
    half = pw_turned_ref[...] * 0.5
    rows = []
    for trace in range(pair):
        held = turned.at[trace]
        held[0:RIM, :] = jnp.zeros((RIM, sources * local), F32)
        total = jnp.zeros((SUBLANES, filters), F32)
        for begin in range(0, length, BLOCK):
            block = x_ref[:, trace, :, begin : begin + BLOCK]
            flipped = block.reshape(sources * local, BLOCK).T.astype(F32)
            value = mixed_half(flipped, begin, dw_turned_ref, half, held)
            silu = value + value * jnp.tanh(value)
            total = total + jnp.sum(silu.reshape(BLOCK // SUBLANES, SUBLANES, filters), 0)
        rows.append(jnp.sum(total, 0, keepdims=True) / length)
    rows = jnp.concatenate(rows, 0).astype(BF16)
    message_ref[...] = jnp.broadcast_to(rows[None], message_ref.shape)


def pool_pass(traces, dw_turned, pw_turned, devices):
    sources, pair, local, length = traces.shape
    metrics, filters = pw_turned.shape
    whole = pl.BlockSpec(memory_space=pltpu.VMEM)
    return pl.pallas_call(
        pool_kernel,
        in_specs=[whole] * 3,
        out_specs=whole,
        out_shape=jax.ShapeDtypeStruct((devices, pair, filters), BF16),
        scratch_shapes=[pltpu.VMEM((pair, length + RIM, metrics), F32)],
        compiler_params=pltpu.CompilerParams(vmem_limit_bytes=8 << 20),
    )(traces, dw_turned, pw_turned)


def terms_kernel(x_ref, dw_turned_ref, pw_turned_ref, terms_ref, turned, slope, plain):
    sources, pair, local, length = x_ref.shape
    metrics = sources * local
    half = pw_turned_ref[...] * 0.5
    for trace in range(pair):
        held, bends, flat = turned, slope, plain
        held[0:RIM, :] = jnp.zeros((RIM, metrics), F32)
        bends[length : length + RIM, :] = jnp.zeros((RIM, bends.shape[1]), BF16)
        for begin in range(0, length, BLOCK):
            block = x_ref[:, trace, :, begin : begin + BLOCK].reshape(metrics, BLOCK)
            flat[:, begin : begin + BLOCK] = block
            value = mixed_half(block.T.astype(F32), begin, dw_turned_ref, half, held)
            bent = jnp.tanh(value)
            bends[begin : begin + BLOCK, :] = (
                (1.0 + bent) * (1.0 + value * (1.0 - bent))
            ).astype(BF16)
        for tap in range(TAPS):
            first = tap * TAP_SPACING
            terms_ref[trace, tap * metrics : (tap + 1) * metrics, :] = jnp.dot(
                flat[...], bends[first : first + length, :], preferred_element_type=F32
            )


def terms_pass(traces, dw_turned, pw_turned):
    sources, pair, local, length = traces.shape
    metrics, filters = pw_turned.shape
    whole = pl.BlockSpec(memory_space=pltpu.VMEM)
    return pl.pallas_call(
        terms_kernel,
        in_specs=[whole] * 3,
        out_specs=whole,
        out_shape=jax.ShapeDtypeStruct((pair, metrics * TAPS, filters), F32),
        scratch_shapes=[
            pltpu.VMEM((length + RIM, metrics), F32),
            pltpu.VMEM((length + RIM, filters), BF16),
            pltpu.VMEM((metrics, length), BF16),
        ],
        compiler_params=pltpu.CompilerParams(vmem_limit_bytes=12 << 20),
    )(traces, dw_turned, pw_turned)


def middle_kernel(
    length, own_ref, pooled_ref, partner_ref, proj_ref, dw_ref, pw_turned_ref, terms_ref,
    loss_ref, grad_proj_ref, sums_ref, losses, held_a, held_v,
):
    filters, width = proj_ref.shape
    count = pooled_ref.shape[0]
    metrics = pw_turned_ref.shape[0]
    factor = LOGIT_SCALE / width
    proj = proj_ref[...]

    def normed(pooled):
        embedding = jnp.dot(pooled, proj, preferred_element_type=F32)
        inverse = lax.rsqrt(jnp.mean(embedding * embedding, 1, keepdims=True) + 1e-06)
        return embedding * inverse, inverse

    unit_a, inverse_a = normed(pooled_ref[:, 0:filters])
    unit_v, inverse_v = normed(pooled_ref[:, filters : 2 * filters])
    queries = unit_a.astype(BF16)
    keys = unit_v.astype(BF16)
    logits = factor * lax.dot_general(
        queries, keys, (((1,), (1,)), ((), ())), preferred_element_type=F32
    )
    columns = lax.broadcasted_iota(jnp.int32, (count, count), 1)
    matches = columns == partner_ref[...]
    weights = jnp.exp(logits - LOGIT_SCALE)
    totals = jnp.sum(weights, 1, keepdims=True)
    positive = jnp.sum(jnp.where(matches, logits, 0.0), 1, keepdims=True)
    losses[...] = LOGIT_SCALE + jnp.log(totals) - positive
    pairs = loss_ref.shape[1]
    first = pl.multiple_of(own_ref[1] * pairs, SUBLANES)
    loss_ref[...] = jnp.broadcast_to(losses[pl.ds(first, pairs), :], (pairs, LANES)).T[0:1, :]
    coeffs = (weights / totals - jnp.where(matches, 1.0, 0.0)).astype(BF16)
    unit_grad_a = factor * jnp.dot(coeffs, keys, preferred_element_type=F32)
    unit_grad_v = factor * lax.dot_general(
        coeffs, queries, (((0,), (0,)), ((), ())), preferred_element_type=F32
    )
    own = own_ref[0]

    def pool_grad(unit, inverse, unit_grad, held):
        grad = inverse * (unit_grad - unit * jnp.mean(unit * unit_grad, 1, keepdims=True))
        grad = grad.astype(BF16)
        held[...] = grad.astype(F32)
        row = jnp.broadcast_to(held[pl.ds(own, 1), :], (16, width)).astype(BF16)
        pool = lax.dot_general(row, proj, (((1,), (1,)), ((), ())), preferred_element_type=F32)
        return pool[0:1, :] * (0.5 / length)

    pool_a = pool_grad(unit_a, inverse_a, unit_grad_a, held_a)
    pool_v = pool_grad(unit_v, inverse_v, unit_grad_v, held_v)

    proj_rows, proj_cols = grad_proj_ref.shape

    def window(ref, begin, first, size):
        lane = pl.multiple_of(begin + first // LANES * LANES, LANES)
        block = ref[:, pl.ds(lane, LANES)].astype(F32)
        return pltpu.roll(block, lax.rem(LANES - lax.rem(first, LANES), LANES), 1).astype(BF16)

    def proj_part(begin, held):
        return lax.dot_general(
            window(pooled_ref, begin, own_ref[2] * proj_rows, proj_rows),
            window(held, 0, own_ref[1] * proj_cols, proj_cols),
            (((0,), (0,)), ((), ())),
            preferred_element_type=F32,
        )

    grad_proj = proj_part(0, held_a) + proj_part(filters, held_v)
    grad_proj_ref[...] = grad_proj[0:proj_rows, 0:proj_cols]

    pw_turned = pw_turned_ref[...].astype(F32)
    lanes = lax.broadcasted_iota(jnp.int32, (metrics, LANES), 1)
    mixing = jnp.zeros((metrics, filters), F32)
    kernel = jnp.zeros((metrics, LANES), F32)
    for tap in range(TAPS):
        rows = pl.ds(tap * metrics, metrics)
        weighted = terms_ref[0, rows, :] * pool_a + terms_ref[1, rows, :] * pool_v
        mixing = mixing + dw_ref[:, tap : tap + 1] * weighted
        column = jnp.sum(pw_turned * weighted, 1, keepdims=True)
        kernel = kernel + jnp.where(lanes == tap, column, 0.0)
    mixing = mixing.T
    kernel = kernel.T
    parts = sums_ref.shape[0]
    mix_rows = filters // parts
    for part in range(parts):
        for row in range(mix_rows):
            sums_ref[part, 0:1, row * LANES : (row + 1) * LANES] = mixing[
                part * mix_rows + row : part * mix_rows + row + 1, :
            ]
        sums_ref[part, 0:1, mix_rows * LANES :] = kernel[part : part + 1, :]


def middle(own, pooled, partners, proj_weight, dw_weight, pw_turned, terms, parts, others, length):
    filters, width = proj_weight.shape
    metrics = pw_turned.shape[0]
    count = pooled.shape[0]
    whole = pl.BlockSpec(memory_space=pltpu.VMEM)
    packed = (filters // parts + 1) * metrics
    return pl.pallas_call(
        functools.partial(middle_kernel, length),
        in_specs=[pl.BlockSpec(memory_space=pltpu.SMEM)] + [whole] * 6,
        out_specs=[whole] * 3,
        out_shape=[
            jax.ShapeDtypeStruct((1, count // parts), F32),
            jax.ShapeDtypeStruct((filters // others, width // parts), F32),
            jax.ShapeDtypeStruct((parts, 1, packed), F32),
        ],
        scratch_shapes=[
            pltpu.VMEM((count, 1), F32),
            pltpu.VMEM((count, width), F32),
            pltpu.VMEM((count, width), F32),
        ],
        compiler_params=pltpu.CompilerParams(vmem_limit_bytes=24 << 20),
    )(own, pooled, partners, proj_weight, dw_weight, pw_turned, terms)


def swap(value, axis):
    return lax.all_to_all(value, axis, 0, 0, tiled=True)


def fold_kernel(parts_ref, out_ref):
    out_ref[...] = jnp.broadcast_to(jnp.sum(parts_ref[...], 0)[None], out_ref.shape)


def fold(parts, copies):
    whole = pl.BlockSpec(memory_space=pltpu.VMEM)
    return pl.pallas_call(
        fold_kernel,
        in_specs=[whole],
        out_specs=whole,
        out_shape=jax.ShapeDtypeStruct((copies,) + parts.shape[1:], F32),
        compiler_params=pltpu.CompilerParams(vmem_limit_bytes=4 << 20),
    )(parts)


def unpack_kernel(index_ref, shares_ref, mix_ref, tap_ref):
    parts = shares_ref.shape[0]
    mix_rows = mix_ref.shape[0] // parts
    taps, local = tap_ref.shape
    for part in range(parts):
        for row in range(mix_rows):
            mix_ref[part * mix_rows + row : part * mix_rows + row + 1, :] = shares_ref[
                part, 0:1, row * LANES : (row + 1) * LANES
            ]
    back = lax.rem(LANES - index_ref[0] * local, LANES)
    rows = jnp.concatenate(
        [shares_ref[tap, 0:1, mix_rows * LANES :] for tap in range(taps)] * (SUBLANES // taps), 0
    )
    tap_ref[...] = pltpu.roll(rows, back, 1)[0:taps, 0:local]


def unpack(chan_index, shares, filters, local_metrics):
    whole = pl.BlockSpec(memory_space=pltpu.VMEM)
    return pl.pallas_call(
        unpack_kernel,
        in_specs=[pl.BlockSpec(memory_space=pltpu.SMEM), whole],
        out_specs=[whole, whole],
        out_shape=[
            jax.ShapeDtypeStruct((filters, LANES), F32),
            jax.ShapeDtypeStruct((TAPS, local_metrics), F32),
        ],
        compiler_params=pltpu.CompilerParams(vmem_limit_bytes=4 << 20),
    )(chan_index.astype(jnp.int32).reshape(1), shares)


def body(anchors, views, dw_weight, pw_weight, proj_weight, partner):
    chan_index = lax.axis_index("chan")
    dp_index = lax.axis_index("dp")
    chan_count = lax.axis_size("chan")
    dp_count = lax.axis_size("dp")
    pairs, local_metrics, length = anchors.shape
    filters, metrics = pw_weight.shape
    width = proj_weight.shape[1]
    dw_turned, pw_turned = dw_weight.T, pw_weight.T

    partners = lax.dynamic_update_slice_in_dim(
        jnp.zeros((dp_count, pairs), jnp.int32), partner[None], dp_index, 0
    )
    bit = 1
    while bit < dp_count:
        partners += lax.ppermute(partners, "dp", [(i, i ^ bit) for i in range(dp_count)])
        bit *= 2
    partners = partners.reshape(pairs * dp_count, 1)
    traces = swap(jnp.stack([anchors, views], 1), "chan")
    traces, partners = lax.optimization_barrier((traces, partners))
    message = pool_pass(traces, dw_turned, pw_turned, dp_count * chan_count)
    pooled = swap(message, ("dp", "chan")).reshape(message.shape[0], -1)
    terms = terms_pass(traces, dw_turned, pw_turned)
    own = jnp.stack([dp_index * chan_count + chan_index, dp_index, chan_index]).astype(jnp.int32)
    loss, grad_proj, sums = middle(
        own, pooled, partners, proj_weight, dw_weight, pw_turned, terms, dp_count, chan_count, length
    )

    shares = fold(swap(sums, "dp"), chan_count)
    shares = fold(swap(shares, "chan"), dp_count)
    grad_pw, grad_dw = unpack(chan_index, swap(shares, "dp"), filters, local_metrics)

    return (loss.reshape(pairs), grad_dw.T, grad_pw, grad_proj)


def solution(mesh):
    placed = (P("dp", "chan", None), P("dp", "chan", None), P(), P(), P(), P("dp"))
    return jax.shard_map(
        body,
        mesh=mesh,
        in_specs=placed,
        out_specs=(P("dp"), P("chan", None), P(), P("chan", "dp")),
        check_vma=False,
    )
```

```python
import functools

import jax
import jax.numpy as jnp
from jax import lax
from jax.experimental import pallas as pl
from jax.experimental.pallas import tpu as pltpu
from jax.sharding import PartitionSpec as P

TAPS = 4
TAP_SPACING = 16
RIM = (TAPS - 1) * TAP_SPACING
LOGIT_SCALE = 16.0
LANES = 128
SUBLANES = 8
BLOCK = 256
F32 = jnp.float32
BF16 = jnp.bfloat16


def mixed_half(flipped, begin, dw_turned_ref, half, turned):
    steps = flipped.shape[0]
    turned[RIM + begin : RIM + begin + steps, :] = flipped
    running = dw_turned_ref[0:1, :] * flipped
    for tap in range(1, TAPS):
        first = RIM + begin - tap * TAP_SPACING
        running = running + dw_turned_ref[tap : tap + 1, :] * turned[first : first + steps, :]
    return jnp.dot(running.astype(BF16), half, preferred_element_type=F32)


def pool_kernel(x_ref, dw_turned_ref, pw_turned_ref, message_ref, turned):
    sources, pair, local, length = x_ref.shape
    filters = pw_turned_ref.shape[1]
    half = pw_turned_ref[...] * 0.5
    rows = []
    for trace in range(pair):
        held = turned.at[trace]
        held[0:RIM, :] = jnp.zeros((RIM, sources * local), F32)
        total = jnp.zeros((SUBLANES, filters), F32)
        for begin in range(0, length, BLOCK):
            block = x_ref[:, trace, :, begin : begin + BLOCK]
            flipped = block.reshape(sources * local, BLOCK).T.astype(F32)
            value = mixed_half(flipped, begin, dw_turned_ref, half, held)
            silu = value + value * jnp.tanh(value)
            total = total + jnp.sum(silu.reshape(BLOCK // SUBLANES, SUBLANES, filters), 0)
        rows.append(jnp.sum(total, 0, keepdims=True) / length)
    rows = jnp.concatenate(rows, 0).astype(BF16)
    message_ref[...] = jnp.broadcast_to(rows[None], message_ref.shape)


def pool_pass(traces, dw_turned, pw_turned, devices):
    sources, pair, local, length = traces.shape
    metrics, filters = pw_turned.shape
    whole = pl.BlockSpec(memory_space=pltpu.VMEM)
    return pl.pallas_call(
        pool_kernel,
        in_specs=[whole] * 3,
        out_specs=whole,
        out_shape=jax.ShapeDtypeStruct((devices, pair, filters), BF16),
        scratch_shapes=[pltpu.VMEM((pair, length + RIM, metrics), F32)],
        compiler_params=pltpu.CompilerParams(vmem_limit_bytes=8 << 20),
    )(traces, dw_turned, pw_turned)


def terms_kernel(x_ref, dw_turned_ref, pw_turned_ref, terms_ref, turned, slope, plain):
    sources, pair, local, length = x_ref.shape
    metrics = sources * local
    half = pw_turned_ref[...] * 0.5
    for trace in range(pair):
        held, bends, flat = turned, slope, plain
        held[0:RIM, :] = jnp.zeros((RIM, metrics), F32)
        bends[length : length + RIM, :] = jnp.zeros((RIM, bends.shape[1]), BF16)
        for begin in range(0, length, BLOCK):
            block = x_ref[:, trace, :, begin : begin + BLOCK].reshape(metrics, BLOCK)
            flat[:, begin : begin + BLOCK] = block
            value = mixed_half(block.T.astype(F32), begin, dw_turned_ref, half, held)
            bent = jnp.tanh(value)
            bends[begin : begin + BLOCK, :] = (
                (1.0 + bent) * (1.0 + value * (1.0 - bent))
            ).astype(BF16)
        for tap in range(TAPS):
            first = tap * TAP_SPACING
            terms_ref[trace, tap * metrics : (tap + 1) * metrics, :] = jnp.dot(
                flat[...], bends[first : first + length, :], preferred_element_type=F32
            )


def terms_pass(traces, dw_turned, pw_turned):
    sources, pair, local, length = traces.shape
    metrics, filters = pw_turned.shape
    whole = pl.BlockSpec(memory_space=pltpu.VMEM)
    return pl.pallas_call(
        terms_kernel,
        in_specs=[whole] * 3,
        out_specs=whole,
        out_shape=jax.ShapeDtypeStruct((pair, metrics * TAPS, filters), F32),
        scratch_shapes=[
            pltpu.VMEM((length + RIM, metrics), F32),
            pltpu.VMEM((length + RIM, filters), BF16),
            pltpu.VMEM((metrics, length), BF16),
        ],
        compiler_params=pltpu.CompilerParams(vmem_limit_bytes=12 << 20),
    )(traces, dw_turned, pw_turned)


def middle_kernel(
    length, own_ref, pooled_ref, partner_ref, proj_ref, dw_ref, pw_turned_ref, terms_ref,
    loss_ref, grad_proj_ref, sums_ref, losses, held_a, held_v,
):
    filters, width = proj_ref.shape
    count = pooled_ref.shape[0]
    metrics = pw_turned_ref.shape[0]
    factor = LOGIT_SCALE / width
    proj = proj_ref[...]

    def normed(pooled):
        embedding = jnp.dot(pooled, proj, preferred_element_type=F32)
        inverse = lax.rsqrt(jnp.mean(embedding * embedding, 1, keepdims=True) + 1e-06)
        return embedding * inverse, inverse

    unit_a, inverse_a = normed(pooled_ref[:, 0:filters])
    unit_v, inverse_v = normed(pooled_ref[:, filters : 2 * filters])
    queries = unit_a.astype(BF16)
    keys = unit_v.astype(BF16)
    logits = factor * lax.dot_general(
        queries, keys, (((1,), (1,)), ((), ())), preferred_element_type=F32
    )
    columns = lax.broadcasted_iota(jnp.int32, (count, count), 1)
    matches = columns == partner_ref[...]
    weights = jnp.exp(logits - LOGIT_SCALE)
    totals = jnp.sum(weights, 1, keepdims=True)
    positive = jnp.sum(jnp.where(matches, logits, 0.0), 1, keepdims=True)
    losses[...] = LOGIT_SCALE + jnp.log(totals) - positive
    pairs = loss_ref.shape[1]
    first = pl.multiple_of(own_ref[1] * pairs, SUBLANES)
    loss_ref[...] = jnp.broadcast_to(losses[pl.ds(first, pairs), :], (pairs, LANES)).T[0:1, :]
    coeffs = (weights / totals - jnp.where(matches, 1.0, 0.0)).astype(BF16)
    unit_grad_a = factor * jnp.dot(coeffs, keys, preferred_element_type=F32)
    unit_grad_v = factor * lax.dot_general(
        coeffs, queries, (((0,), (0,)), ((), ())), preferred_element_type=F32
    )
    own = own_ref[0]

    def pool_grad(unit, inverse, unit_grad, held):
        grad = inverse * (unit_grad - unit * jnp.mean(unit * unit_grad, 1, keepdims=True))
        grad = grad.astype(BF16)
        held[...] = grad.astype(F32)
        row = jnp.broadcast_to(held[pl.ds(own, 1), :], (16, width)).astype(BF16)
        pool = lax.dot_general(row, proj, (((1,), (1,)), ((), ())), preferred_element_type=F32)
        return pool[0:1, :] * (0.5 / length)

    pool_a = pool_grad(unit_a, inverse_a, unit_grad_a, held_a)
    pool_v = pool_grad(unit_v, inverse_v, unit_grad_v, held_v)

    proj_rows, proj_cols = grad_proj_ref.shape

    def window(ref, begin, first, size):
        lane = pl.multiple_of(begin + first // LANES * LANES, LANES)
        block = ref[:, pl.ds(lane, LANES)].astype(F32)
        return pltpu.roll(block, lax.rem(LANES - lax.rem(first, LANES), LANES), 1).astype(BF16)

    def proj_part(begin, held):
        return lax.dot_general(
            window(pooled_ref, begin, own_ref[2] * proj_rows, proj_rows),
            window(held, 0, own_ref[1] * proj_cols, proj_cols),
            (((0,), (0,)), ((), ())),
            preferred_element_type=F32,
        )

    grad_proj = proj_part(0, held_a) + proj_part(filters, held_v)
    grad_proj_ref[...] = grad_proj[0:proj_rows, 0:proj_cols]

    pw_turned = pw_turned_ref[...].astype(F32)
    lanes = lax.broadcasted_iota(jnp.int32, (metrics, LANES), 1)
    mixing = jnp.zeros((metrics, filters), F32)
    kernel = jnp.zeros((metrics, LANES), F32)
    for tap in range(TAPS):
        rows = pl.ds(tap * metrics, metrics)
        weighted = terms_ref[0, rows, :] * pool_a + terms_ref[1, rows, :] * pool_v
        mixing = mixing + dw_ref[:, tap : tap + 1] * weighted
        column = jnp.sum(pw_turned * weighted, 1, keepdims=True)
        kernel = kernel + jnp.where(lanes == tap, column, 0.0)
    mixing = mixing.T
    kernel = kernel.T
    parts = sums_ref.shape[0]
    mix_rows = filters // parts
    for part in range(parts):
        for row in range(mix_rows):
            sums_ref[part, 0:1, row * LANES : (row + 1) * LANES] = mixing[
                part * mix_rows + row : part * mix_rows + row + 1, :
            ]
        sums_ref[part, 0:1, mix_rows * LANES :] = kernel[part : part + 1, :]


def middle(own, pooled, partners, proj_weight, dw_weight, pw_turned, terms, parts, others, length):
    filters, width = proj_weight.shape
    metrics = pw_turned.shape[0]
    count = pooled.shape[0]
    whole = pl.BlockSpec(memory_space=pltpu.VMEM)
    packed = (filters // parts + 1) * metrics
    return pl.pallas_call(
        functools.partial(middle_kernel, length),
        in_specs=[pl.BlockSpec(memory_space=pltpu.SMEM)] + [whole] * 6,
        out_specs=[whole] * 3,
        out_shape=[
            jax.ShapeDtypeStruct((1, count // parts), F32),
            jax.ShapeDtypeStruct((filters // others, width // parts), F32),
            jax.ShapeDtypeStruct((parts, 1, packed), F32),
        ],
        scratch_shapes=[
            pltpu.VMEM((count, 1), F32),
            pltpu.VMEM((count, width), F32),
            pltpu.VMEM((count, width), F32),
        ],
        compiler_params=pltpu.CompilerParams(vmem_limit_bytes=24 << 20),
    )(own, pooled, partners, proj_weight, dw_weight, pw_turned, terms)


def swap(value, axis):
    return lax.all_to_all(value, axis, 0, 0, tiled=True)


def fold_kernel(parts_ref, out_ref):
    out_ref[...] = jnp.broadcast_to(jnp.sum(parts_ref[...], 0)[None], out_ref.shape)


def fold(parts, copies):
    whole = pl.BlockSpec(memory_space=pltpu.VMEM)
    return pl.pallas_call(
        fold_kernel,
        in_specs=[whole],
        out_specs=whole,
        out_shape=jax.ShapeDtypeStruct((copies,) + parts.shape[1:], F32),
        compiler_params=pltpu.CompilerParams(vmem_limit_bytes=4 << 20),
    )(parts)


def unpack_kernel(index_ref, shares_ref, mix_ref, tap_ref):
    parts = shares_ref.shape[0]
    mix_rows = mix_ref.shape[0] // parts
    taps, local = tap_ref.shape
    for part in range(parts):
        for row in range(mix_rows):
            mix_ref[part * mix_rows + row : part * mix_rows + row + 1, :] = shares_ref[
                part, 0:1, row * LANES : (row + 1) * LANES
            ]
    back = lax.rem(LANES - index_ref[0] * local, LANES)
    rows = jnp.concatenate(
        [shares_ref[tap, 0:1, mix_rows * LANES :] for tap in range(taps)] * (SUBLANES // taps), 0
    )
    tap_ref[...] = pltpu.roll(rows, back, 1)[0:taps, 0:local]


def unpack(chan_index, shares, filters, local_metrics):
    whole = pl.BlockSpec(memory_space=pltpu.VMEM)
    return pl.pallas_call(
        unpack_kernel,
        in_specs=[pl.BlockSpec(memory_space=pltpu.SMEM), whole],
        out_specs=[whole, whole],
        out_shape=[
            jax.ShapeDtypeStruct((filters, LANES), F32),
            jax.ShapeDtypeStruct((TAPS, local_metrics), F32),
        ],
        compiler_params=pltpu.CompilerParams(vmem_limit_bytes=4 << 20),
    )(chan_index.astype(jnp.int32).reshape(1), shares)


def body(anchors, views, dw_weight, pw_weight, proj_weight, partner):
    chan_index = lax.axis_index("chan")
    dp_index = lax.axis_index("dp")
    chan_count = lax.axis_size("chan")
    dp_count = lax.axis_size("dp")
    pairs, local_metrics, length = anchors.shape
    filters, metrics = pw_weight.shape
    width = proj_weight.shape[1]
    dw_turned, pw_turned = dw_weight.T, pw_weight.T

    partners = lax.dynamic_update_slice_in_dim(
        jnp.zeros((dp_count, pairs), jnp.int32), partner[None], dp_index, 0
    )
    bit = 1
    while bit < dp_count:
        partners += lax.ppermute(partners, "dp", [(i, i ^ bit) for i in range(dp_count)])
        bit *= 2
    partners = partners.reshape(pairs * dp_count, 1)
    traces = swap(jnp.stack([anchors, views], 1), "chan")
    traces, partners = lax.optimization_barrier((traces, partners))
    message = pool_pass(traces, dw_turned, pw_turned, dp_count * chan_count)
    pooled = swap(message, ("dp", "chan")).reshape(message.shape[0], -1)
    terms = terms_pass(traces, dw_turned, pw_turned)
    own = jnp.stack([dp_index * chan_count + chan_index, dp_index, chan_index]).astype(jnp.int32)
    loss, grad_proj, sums = middle(
        own, pooled, partners, pltpu.with_memory_space_constraint(proj_weight, pltpu.HBM), dw_weight,
        pw_turned, terms, dp_count, chan_count, length,
    )

    shares = fold(swap(sums, "dp"), chan_count)
    shares = fold(swap(shares, "chan"), dp_count)
    grad_pw, grad_dw = unpack(chan_index, swap(shares, "dp"), filters, local_metrics)

    return (loss.reshape(pairs), grad_dw.T, grad_pw, grad_proj)


def solution(mesh):
    placed = (P("dp", "chan", None), P("dp", "chan", None), P(), P(), P(), P("dp"))
    return jax.shard_map(
        body,
        mesh=mesh,
        in_specs=placed,
        out_specs=(P("dp"), P("chan", None), P(), P("chan", "dp")),
        check_vma=False,
    )
```
